32 devices in a mesh: dp: 4 (over z), row: 2 (over x), col: 4 (over y, core).
Axes of the slice: x: 2, y: 2, z: 4, core: 2. Of those that a mesh axis runs over, the one named last changes fastest.
Arguments:
- layer_input_rows: float32 [1024, 1024], P('dp', ('row', 'col')), may hold values from -6 to 6
- first_layer_values: float32 [1024, 1024], P('dp', ('col', 'row')), may hold values from -6 to 6
- document_index: int32 [4, 256], P('dp'), may hold values from 0 to 3, never falling along the last dimension, each value on 1 to 128 neighbouring positions
- output_cotangent: float32 [1024, 1024], P('dp', ('row', 'col')), may hold values from -6 to 6
- feature_parameters: float32 [11, 1024], P(None, ('row', 'col')), may hold values from -0.5 to 1.5, as said below
- head_parameters: float32 [8, 1024], P(None, ('col', 'row')), may hold values from -8 to 1.5, as said below
- receptance_weight: bfloat16 [1024, 1024], P('row', 'col'), may hold values from -0.1875 to 0.1875
- key_weight: bfloat16 [1024, 1024], P('row', 'col'), may hold values from -0.1875 to 0.1875
- value_weight: bfloat16 [1024, 1024], P('row', 'col'), may hold values from -0.1875 to 0.1875
- output_weight: bfloat16 [1024, 1024], P('col', 'row'), may hold values from -0.1875 to 0.1875
- channel_key_weight: bfloat16 [1024, 4096], P('row', 'col'), may hold values from -0.1875 to 0.1875
- channel_value_weight: bfloat16 [4096, 1024], P('col', 'row'), may hold values from -0.09375 to 0.09375
- down_factors: bfloat16 [1024, 320], P(('row', 'col')), may hold values from -0.1875 to 0.1875
- up_factors: bfloat16 [320, 1024], P(None, ('col', 'row')), may hold values from -0.75 to 0.75
Outputs:
- block_out: float32 [1024, 1024], P('dp', ('row', 'col'))
- input_grad: float32 [1024, 1024], P('dp', ('row', 'col'))
- value_first_grad: float32 [1024, 1024], P('dp', ('col', 'row'))
- feature_gradient: float32 [11, 1024], P(None, ('row', 'col'))
- head_parameter_gradient: float32 [8, 1024], P(None, ('col', 'row'))
- grad_recep: float32 [1024, 1024], P('row', 'col')
- grad_key: float32 [1024, 1024], P('row', 'col')
- grad_value: float32 [1024, 1024], P('row', 'col')
- output_weight_gradient: float32 [1024, 1024], P('col', 'row')
- channel_key_gradient: float32 [1024, 4096], P('row', 'col')
- channel_value_gradient: float32 [4096, 1024], P('col', 'row')
- down_factor_gradient: float32 [1024, 320], P(('row', 'col'))
- up_factor_gradient: float32 [320, 1024], P(None, ('col', 'row'))
The draws below stay inside these ranges and needn't reach their ends.
Inputs may be any that keep to these rules, and one draw needn't show every extreme that they name: Each row of document_index is one pack of 256 tokens; document numbers never fall along a row, and no document continues into another row. `feature_parameters`: rows 0 and 2 lie within 0.5 to 1.5, rows 1 and 3 within -0.5 to 0.5, rows 4 to 10 within 0 to 1. `head_parameters`: row 0 lies within -8 to 1, rows 1 and 2 within -1.5 to 1.5, rows 3, 6 within 0.5 to 1.5, row 4 within 0 to 1.5, rows 5 and 7 within -1 to 1.
All inputs are finite; a program needn't handle non-finite values.
Results may differ from the reference program's by a relative error of at most 0.035.
Values may be sent and summed in bfloat16 or wider, within the bound.
No kernel may reach another device: no remote copies, remote signals or barrier semaphores. Data moves between devices by JAX's collectives and lax.ppermute only.
A program may use at most 256 MiB of HBM per device.

```python
import math
import jax
import jax.numpy as jnp
import numpy as np
from jax import lax

EMBED_SIZE = 1024
HEAD = 64
FF = 4096
LOWRANK_DECAY = 64
LOWRANK_RATE = 64
LOWRANK_VALUE = 32
LOWRANK_GATE = 160
LOWRANK_TOTAL = 320
TOK_DEV = 256
DOCS = 4
PACKS = 4
TOKENS = 1024


def draw_feature_parameters(key, part):
    lookup_matrix_lines = jax.random.split(jax.random.fold_in(key, 11), 3)
    gains = jax.random.uniform(lookup_matrix_lines[0], (2, EMBED_SIZE), jnp.float32, 0.6, 1.4)
    biases = jax.random.uniform(lookup_matrix_lines[1], (2, EMBED_SIZE), jnp.float32, -0.4, 0.4)
    mixes = jax.random.uniform(lookup_matrix_lines[2], (7, EMBED_SIZE), jnp.float32, 0.05, 0.95)
    head_rows = jnp.stack([gains[0], biases[0], gains[1], biases[1]])
    return jnp.concatenate([head_rows, mixes], axis=0)


def draw_head_parameters(key, part):
    lookup_matrix_lines = jax.random.split(jax.random.fold_in(key, 23), 8)
    forgetting_shift_vector = jax.random.uniform(lookup_matrix_lines[0], (EMBED_SIZE,), jnp.float32, -6.0, 1.0)
    learning_shift_vector = jax.random.uniform(lookup_matrix_lines[1], (EMBED_SIZE,), jnp.float32, -1.0, 1.0)
    content_shift_vector = jax.random.uniform(lookup_matrix_lines[2], (EMBED_SIZE,), jnp.float32, -1.0, 1.0)
    lookup_unitize_multiplier = jax.random.uniform(lookup_matrix_lines[3], (EMBED_SIZE,), jnp.float32, 0.5, 1.5)
    lookup_learning_multiplier = jax.random.uniform(lookup_matrix_lines[4], (EMBED_SIZE,), jnp.float32, 0.0, 1.5)
    reward_coefficient_vector = jax.random.uniform(lookup_matrix_lines[5], (EMBED_SIZE,), jnp.float32, -1.0, 1.0)
    cluster_standardize_multiplier = jax.random.uniform(lookup_matrix_lines[6], (EMBED_SIZE,), jnp.float32, 0.5, 1.5)
    cluster_standardize_shift = jax.random.uniform(lookup_matrix_lines[7], (EMBED_SIZE,), jnp.float32, -1.0, 1.0)
    return jnp.stack([forgetting_shift_vector, learning_shift_vector, content_shift_vector, lookup_unitize_multiplier, lookup_learning_multiplier, reward_coefficient_vector, cluster_standardize_multiplier, cluster_standardize_shift])


def shard_levels(own_key, dims, cuts, smallest, high):
    def one(dim, parts):
        steps = jax.random.uniform(jax.random.fold_in(jax.random.fold_in(own_key, 6), dim), (parts,), jnp.float32, smallest / len(cuts), high / len(cuts))
        return jnp.repeat(jnp.exp(steps), dims[dim] // parts).reshape((-1,) + (1,) * (len(dims) - dim - 1))

    level = one(*cuts[0])
    for cut in cuts[1:]:
        level = level * one(*cut)
    return level


def length_profile(count, total, most, slope):
    weights = [(1 << 20) // math.isqrt(standing ** slope) + 1 for standing in range(2, count + 1)]
    spare, counts = total - most - (count - 1), [1] * (count - 1)
    while spare > 0:
        movable = [i for i in range(count - 1) if counts[i] < most]
        mass, remaining = sum([weights[i] for i in movable]), spare
        for i in movable:
            more = min(most - counts[i], max(1, remaining * weights[i] // mass), spare)
            counts[i] = counts[i] + more
            spare = spare - more
    return np.array([most] + counts)


def uneven_parts(key, number_of, total, bound, lean):
    if number_of == 2:
        one = jax.random.randint(key, (), max(1, total - bound), min(bound, total - 1) + 1)
        return jnp.stack([one, total - one])
    sizes = jnp.asarray(length_profile(number_of, total, bound, lean), jnp.int32)
    couples = (number_of - 1) // 2
    donor, taker = sizes[1:1 + 2 * couples:2], sizes[2:2 + 2 * couples:2]
    slack = jnp.minimum(donor - 1, bound - taker)
    shifted = jax.random.randint(jax.random.fold_in(key, 1), (couples,), 0, 1 << 20) % (slack + 1)
    sizes = sizes.at[1:1 + 2 * couples:2].set(donor - shifted).at[2:2 + 2 * couples:2].set(taker + shifted)
    return sizes[jax.random.permutation(jax.random.fold_in(key, 2), number_of)]


def bell_draw(stream_key, extent, scale, bound, cuts=(), kind=jnp.bfloat16):
    array = scale * jax.random.normal(stream_key, extent, jnp.float32)
    if cuts:
        array = array * shard_levels(stream_key, extent, cuts, -0.22, 0.18)
    return jnp.clip(array, -bound, bound).astype(kind)


def setup_inputs(seed: int = 0) -> dict:
    key_list = jax.random.split(jax.random.key(seed), 15)
    layer_input_rows = bell_draw(key_list[0], (TOKENS, EMBED_SIZE), 1.0, 6.0, ((0, 4), (1, 8)), jnp.float32)
    first_layer_values = bell_draw(key_list[1], (TOKENS, EMBED_SIZE), 1.0, 6.0, ((0, 4), (1, 8)), jnp.float32)
    document_index = jax.vmap(lambda own: jnp.searchsorted(jnp.cumsum(uneven_parts(own, DOCS, TOK_DEV, TOK_DEV // 2, 1)), jnp.arange(TOK_DEV), side="right"))(jax.random.split(key_list[2], PACKS)).reshape((PACKS, TOK_DEV)).astype(jnp.int32)
    output_cotangent = bell_draw(key_list[3], (TOKENS, EMBED_SIZE), 1.0, 6.0, ((0, 4), (1, 8)), jnp.float32)
    feature_parameters = draw_feature_parameters(jax.random.fold_in(key_list[14], 71), 0)
    head_parameters = draw_head_parameters(jax.random.fold_in(key_list[14], 71), 0)
    receptance_weight = bell_draw(key_list[6], (EMBED_SIZE, EMBED_SIZE), EMBED_SIZE ** -0.5, 0.1875, ((0, 2), (1, 4)))
    key_weight = bell_draw(key_list[7], (EMBED_SIZE, EMBED_SIZE), EMBED_SIZE ** -0.5, 0.1875, ((0, 2), (1, 4)))
    value_weight = bell_draw(key_list[8], (EMBED_SIZE, EMBED_SIZE), EMBED_SIZE ** -0.5, 0.1875, ((0, 2), (1, 4)))
    output_weight = bell_draw(key_list[9], (EMBED_SIZE, EMBED_SIZE), EMBED_SIZE ** -0.5, 0.1875, ((0, 4), (1, 2)))
    channel_key_weight = bell_draw(key_list[10], (EMBED_SIZE, FF), EMBED_SIZE ** -0.5, 0.1875, ((0, 2), (1, 4)))
    channel_value_weight = bell_draw(key_list[11], (FF, EMBED_SIZE), FF ** -0.5, 0.09375, ((0, 4), (1, 2)))
    down_factors = bell_draw(key_list[12], (EMBED_SIZE, LOWRANK_TOTAL), EMBED_SIZE ** -0.5, 0.1875, ((0, 8),))
    up_factors = bell_draw(key_list[13], (LOWRANK_TOTAL, EMBED_SIZE), LOWRANK_DECAY ** -0.5, 0.75, ((1, 8),))
    return {"layer_input_rows": layer_input_rows, "first_layer_values": first_layer_values, "document_index": document_index, "output_cotangent": output_cotangent, "feature_parameters": feature_parameters, "head_parameters": head_parameters, "receptance_weight": receptance_weight, "key_weight": key_weight, "value_weight": value_weight, "output_weight": output_weight, "channel_key_weight": channel_key_weight, "channel_value_weight": channel_value_weight, "down_factors": down_factors, "up_factors": up_factors}


ln_eps = 1e-05
gn_eps = 1.0
key_eps = 1e-06
highest = lax.Precision.HIGHEST

def plain_timing(left, right):
    return jnp.dot(left, right, preferred_element_type=jnp.float32)

def backward_timing(left, right):
    return lax.dot_general(left, right, (((1,), (1,)), ((), ())), preferred_element_type=jnp.float32)

def outer_timing(left, right):
    return lax.dot_general(left, right, (((0,), (0,)), ((), ())), preferred_element_type=jnp.float32)

def norm_forward(values, gain, bias):
    center = lax.optimization_barrier(jnp.mean(values, axis=1, keepdims=True))
    squares = lax.optimization_barrier(jnp.mean(values * values, axis=1, keepdims=True))
    inv_std = lax.rsqrt(squares - center * center + ln_eps)
    scaled = (values - center) * inv_std
    return (scaled * gain + bias, scaled, inv_std)

def norm_backward(grad_out, scaled, inv_std, gain):
    grad_scaled = grad_out * gain
    first_mean = lax.optimization_barrier(jnp.mean(grad_scaled, axis=1, keepdims=True))
    second_mean = lax.optimization_barrier(jnp.mean(grad_scaled * scaled, axis=1, keepdims=True))
    return (grad_scaled - first_mean - scaled * second_mean) * inv_std

def shift_prev(values, same_doc):
    moved = jnp.concatenate([jnp.zeros_like(values[:1]), values[:-1]], axis=0)
    return moved * same_doc[:, None]

def shift_next(values, same_doc):
    weighted = values * same_doc[:, None]
    return jnp.concatenate([weighted[1:], jnp.zeros_like(values[:1])], axis=0)

def mixer_inputs(receptance, key_raw, value_raw, first_value, decay_low, rate_low, value_low, attention_unit_settings):
    sequence_length, embedding_dimension = key_raw.shape
    attention_partition = embedding_dimension // HEAD

    def split_heads(values):
        return values.reshape(sequence_length, attention_partition, HEAD)
    log_decay = -jax.nn.softplus(-(attention_unit_settings[0] + decay_low)) - 0.5
    decay = jnp.exp(-jnp.exp(log_decay))
    in_rate = jax.nn.sigmoid(attention_unit_settings[1] + rate_low)
    value = value_raw + (first_value - value_raw) * jax.nn.sigmoid(attention_unit_settings[2] + value_low)
    key_norm = split_heads(key_raw * attention_unit_settings[3])
    key_norm = key_norm * lax.rsqrt(lax.optimization_barrier(jnp.sum(key_norm * key_norm, axis=2, keepdims=True)) + key_eps)
    key_used = key_raw * (1.0 + (in_rate - 1.0) * attention_unit_settings[4])
    return (split_heads(receptance), split_heads(decay), key_norm, key_norm * split_heads(in_rate), split_heads(value), split_heads(key_used))

def mixer_output(state_out, acceptance_partitioned, lookup_vectors_partitioned, content_partitioned, result_sigmoid_mask, attention_unit_settings):
    sequence_length, attention_partition, embedding_dimension = state_out.shape
    center = lax.optimization_barrier(jnp.mean(state_out, axis=2, keepdims=True))
    spread = lax.optimization_barrier(jnp.mean(jnp.square(state_out - center), axis=2, keepdims=True))
    standardized_source = ((state_out - center) * lax.rsqrt(spread + gn_eps)).reshape(sequence_length, attention_partition * embedding_dimension)
    extra_reward_summand = lax.optimization_barrier(jnp.sum(acceptance_partitioned * lookup_vectors_partitioned * attention_unit_settings[5].reshape(attention_partition, embedding_dimension), axis=2, keepdims=True)) * content_partitioned
    return (standardized_source * attention_unit_settings[6] + attention_unit_settings[7] + extra_reward_summand.reshape(sequence_length, attention_partition * embedding_dimension)) * result_sigmoid_mask

def recurrence(acceptance_partitioned, decay, key_norm, lookup_learning_multiplier, content_partitioned, lookup_vectors_partitioned, same_doc):
    sequence_length, attention_partition, embedding_dimension = acceptance_partitioned.shape

    def advance(state, current):
        recep_now, decay_now, norm_now, rate_now, value_now, key_now, keep_now = current
        state = state * keep_now
        removed = jnp.einsum('hvk,hk->hv', state, norm_now, precision=highest)
        state = state * decay_now[:, None, :] - removed[:, :, None] * rate_now[:, None, :] + value_now[:, :, None] * key_now[:, None, :]
        return (state, jnp.einsum('hvk,hk->hv', state, recep_now, precision=highest))
    start = jnp.zeros((attention_partition, embedding_dimension, embedding_dimension), jnp.float32)
    _, outputs = lax.scan(advance, start, (acceptance_partitioned, decay, key_norm, lookup_learning_multiplier, content_partitioned, lookup_vectors_partitioned, same_doc))
    return outputs

def time_mix(receptance, key_raw, value_raw, first_value, decay_low, rate_low, value_low, result_sigmoid_mask, attention_unit_settings, same_doc):
    acceptance_partitioned, decay, key_norm, lookup_learning_multiplier, content_partitioned, lookup_vectors_partitioned = mixer_inputs(receptance, key_raw, value_raw, first_value, decay_low, rate_low, value_low, attention_unit_settings)
    state_out = recurrence(acceptance_partitioned, decay, key_norm, lookup_learning_multiplier, content_partitioned, lookup_vectors_partitioned, same_doc)
    return mixer_output(state_out, acceptance_partitioned, lookup_vectors_partitioned, content_partitioned, result_sigmoid_mask, attention_unit_settings)

def one_pack(weight_list, layer_input_rows, first_layer_values, docs, output_cotangent):
    feature_parameters, head_parameters, receptance_weight, key_weight, value_weight, output_weight, channel_key_weight, channel_value_weight, down_factors, up_factors = weight_list
    same_doc = jnp.concatenate([jnp.zeros((1,), jnp.float32), (docs[1:] == docs[:-1]).astype(jnp.float32)])
    normed_one, scaled_one, inv_one = norm_forward(layer_input_rows, feature_parameters[0], feature_parameters[1])
    delta_one = shift_prev(normed_one, same_doc) - normed_one
    time_mixes = feature_parameters[4:10]
    mixed_all = (normed_one[:, None, :] + delta_one[:, None, :] * time_mixes[None]).astype(jnp.bfloat16)
    proj_weights = (receptance_weight, key_weight, value_weight)
    projected = [plain_timing(mixed_all[:, position_index], proj_weights[position_index]) for position_index in range(3)]
    border_first = LOWRANK_DECAY
    border_second = border_first + LOWRANK_RATE
    border_third = border_second + LOWRANK_VALUE
    border_fourth = border_third + LOWRANK_GATE
    segment_bounds = ((0, border_first), (border_first, border_second), (border_second, border_third), (border_third, border_fourth))
    lowrank_inputs = (mixed_all[:, 3], mixed_all[:, 4], mixed_all[:, 2], mixed_all[:, 5])
    hidden_activation = jnp.concatenate([plain_timing(lowrank_inputs[position_index], down_factors[:, segment_bounds[position_index][0]:segment_bounds[position_index][1]]) for position_index in range(4)], axis=1)
    pieces = [hidden_activation[:, segment_bounds[position_index][0]:segment_bounds[position_index][1]] for position_index in range(4)]
    acts_full = [jnp.tanh(pieces[0]), pieces[1], pieces[2], jax.nn.sigmoid(pieces[3])]
    layer_activations = [piece.astype(jnp.bfloat16) for piece in acts_full]
    lowrank_outputs = [plain_timing(layer_activations[position_index], up_factors[segment_bounds[position_index][0]:segment_bounds[position_index][1]]) for position_index in range(4)]

    def mixer_fn(receptance, key_raw, value_raw, first_value, decay_low, rate_low, value_low, result_sigmoid_mask, attention_unit_settings):
        return time_mix(receptance, key_raw, value_raw, first_value, decay_low, rate_low, value_low, result_sigmoid_mask, attention_unit_settings, same_doc)
    core, core_back = jax.vjp(mixer_fn, projected[0], projected[1], projected[2], first_layer_values, lowrank_outputs[0], lowrank_outputs[1], lowrank_outputs[2], lowrank_outputs[3], head_parameters)
    core_half = core.astype(jnp.bfloat16)
    residual_one = layer_input_rows + plain_timing(core_half, output_weight)
    normed_two, scaled_two, inv_two = norm_forward(residual_one, feature_parameters[2], feature_parameters[3])
    delta_two = shift_prev(normed_two, same_doc) - normed_two
    ffn_input = (normed_two + delta_two * feature_parameters[10]).astype(jnp.bfloat16)
    pre_act = plain_timing(ffn_input, channel_key_weight)
    hidden_act = jnp.square(jax.nn.relu(pre_act)).astype(jnp.bfloat16)
    block_out = residual_one + plain_timing(hidden_act, channel_value_weight)
    grad_half = output_cotangent.astype(jnp.bfloat16)
    channel_value_gradient = outer_timing(hidden_act, grad_half)
    grad_hidden = backward_timing(grad_half, channel_value_weight)
    grad_pre = (2.0 * grad_hidden * jax.nn.relu(pre_act)).astype(jnp.bfloat16)
    channel_key_gradient = outer_timing(ffn_input, grad_pre)
    grad_ffn_in = backward_timing(grad_pre, channel_key_weight)
    grad_mix_ffn = lax.optimization_barrier(jnp.sum(grad_ffn_in * delta_two, axis=0))
    grad_normed_two = grad_ffn_in * (1.0 - feature_parameters[10]) + shift_next(grad_ffn_in * feature_parameters[10], same_doc)
    grad_gain_two = lax.optimization_barrier(jnp.sum(grad_normed_two * scaled_two, axis=0))
    grad_bias_two = lax.optimization_barrier(jnp.sum(grad_normed_two, axis=0))
    grad_residual = output_cotangent + norm_backward(grad_normed_two, scaled_two, inv_two, feature_parameters[2])
    residual_half = grad_residual.astype(jnp.bfloat16)
    output_weight_gradient = outer_timing(core_half, residual_half)
    grad_core = backward_timing(residual_half, output_weight)
    back_terms = core_back(grad_core)
    value_first_grad = back_terms[3]
    head_parameter_gradient = back_terms[8]
    lowrank_halfway = [back_terms[4 + position_index].astype(jnp.bfloat16) for position_index in range(4)]
    up_factor_gradient = jnp.concatenate([outer_timing(layer_activations[position_index], lowrank_halfway[position_index]) for position_index in range(4)], axis=0)
    lowrank_hidden_gradient = [backward_timing(lowrank_halfway[position_index], up_factors[segment_bounds[position_index][0]:segment_bounds[position_index][1]]) for position_index in range(4)]
    lowrank_hidden_gradient[0] = lowrank_hidden_gradient[0] * (1.0 - acts_full[0] * acts_full[0])
    lowrank_hidden_gradient[3] = lowrank_hidden_gradient[3] * acts_full[3] * (1.0 - acts_full[3])
    hidden_halfway = [piece.astype(jnp.bfloat16) for piece in lowrank_hidden_gradient]
    down_factor_gradient = jnp.concatenate([outer_timing(lowrank_inputs[position_index], hidden_halfway[position_index]) for position_index in range(4)], axis=1)
    lowrank_input_gradient = [backward_timing(hidden_halfway[position_index], down_factors[:, segment_bounds[position_index][0]:segment_bounds[position_index][1]]) for position_index in range(4)]
    rkv_half = [back_terms[position_index].astype(jnp.bfloat16) for position_index in range(3)]
    projection_gradient = [outer_timing(mixed_all[:, position_index], rkv_half[position_index]) for position_index in range(3)]
    grad_proj_in = [backward_timing(rkv_half[position_index], proj_weights[position_index]) for position_index in range(3)]
    grad_mixed = jnp.stack([grad_proj_in[0], grad_proj_in[1], grad_proj_in[2] + lowrank_input_gradient[2], lowrank_input_gradient[0], lowrank_input_gradient[1], lowrank_input_gradient[3]], axis=1)
    grad_mixes = lax.optimization_barrier(jnp.sum(grad_mixed * delta_one[:, None, :], axis=0))
    grad_normed_one = lax.optimization_barrier(jnp.sum(grad_mixed * (1.0 - time_mixes[None]), axis=1)) + shift_next(lax.optimization_barrier(jnp.sum(grad_mixed * time_mixes[None], axis=1)), same_doc)
    grad_gain_one = lax.optimization_barrier(jnp.sum(grad_normed_one * scaled_one, axis=0))
    grad_bias_one = lax.optimization_barrier(jnp.sum(grad_normed_one, axis=0))
    input_grad = grad_residual + norm_backward(grad_normed_one, scaled_one, inv_one, feature_parameters[0])
    feature_gradient = jnp.concatenate([jnp.stack([grad_gain_one, grad_bias_one, grad_gain_two, grad_bias_two]), grad_mixes, grad_mix_ffn[None]], axis=0)
    gradient_list = (feature_gradient, head_parameter_gradient, projection_gradient[0], projection_gradient[1], projection_gradient[2], output_weight_gradient, channel_key_gradient, channel_value_gradient, down_factor_gradient, up_factor_gradient)
    return ((block_out, input_grad, value_first_grad), gradient_list)

def reference(layer_input_rows, first_layer_values, document_index, output_cotangent, feature_parameters, head_parameters, receptance_weight, key_weight, value_weight, output_weight, channel_key_weight, channel_value_weight, down_factors, up_factors):
    packs = document_index.shape[0]
    sequence_length = document_index.shape[1]
    weight_list = (feature_parameters, head_parameters, receptance_weight, key_weight, value_weight, output_weight, channel_key_weight, channel_value_weight, down_factors, up_factors)

    def to_packs(values):
        return values.reshape(packs, sequence_length, values.shape[1])
    start = tuple((jnp.zeros(weight.shape, jnp.float32) for weight in weight_list))

    def advance(totals, pack):
        outputs, gradient_list = one_pack(weight_list, pack[0], pack[1], pack[2], pack[3])
        return (tuple((total + grad for total, grad in zip(totals, gradient_list))), outputs)
    totals, outputs = lax.scan(advance, start, (to_packs(layer_input_rows), to_packs(first_layer_values), document_index, to_packs(output_cotangent)))
    flat = [output.reshape(packs * sequence_length, output.shape[2]) for output in outputs]
    return (flat[0], flat[1], flat[2], totals[0], totals[1], totals[2], totals[3], totals[4], totals[5], totals[6], totals[7], totals[8], totals[9])
```

```python
import jax
import jax.numpy as jnp
from jax import lax
from jax.experimental import pallas as pl
from jax.experimental.pallas import tpu as pltpu
from jax.sharding import PartitionSpec as P

EMBED_SIZE = 1024
LOWRANK_DECAY = 64
LOWRANK_RATE = 64
LOWRANK_VALUE = 32
LOWRANK_GATE = 160
ln_eps = 1e-05
HEAD = 64
gn_eps = 1.0
key_eps = 1e-06
decay_scale = 0.6065306597126334
interpreted = False


def split_two(values):
    high = values.astype(jnp.bfloat16)
    return high, (values - high.astype(jnp.float32)).astype(jnp.bfloat16)


def dims(left, right):
    return (((left,), (right,)), ((), ()))


def dot_fine(left, right, numbers):
    left_high, left_low = left
    right_high, right_low = right

    def one(a, b):
        return lax.dot_general(a, b, numbers, preferred_element_type=jnp.float32)

    return one(left_high, right_high) + (one(left_high, right_low) + one(left_low, right_high))


def head_ones(width):
    rows = lax.broadcasted_iota(jnp.int32, (width, width), 0) // HEAD
    cols = lax.broadcasted_iota(jnp.int32, (width, width), 1) // HEAD
    return (rows == cols).astype(jnp.bfloat16)


def raw_head_sums(values):
    ones = head_ones(values.shape[1])
    high, low = split_two(values)
    numbers = dims(1, 0)
    return lax.dot_general(
        high, ones, numbers, preferred_element_type=jnp.float32
    ) + lax.dot_general(low, ones, numbers, preferred_element_type=jnp.float32)


@jax.custom_vjp
def head_sums(values):
    return raw_head_sums(values)


head_sums.defvjp(lambda values: (raw_head_sums(values), None), lambda _, grad: (raw_head_sums(grad),))


def sigmoid(values):
    return 1.0 / (1.0 + jnp.exp(-values))


def mixer_inputs(key_raw, value_raw, first_value, decay_low, rate_low, value_low, p0, p1, p2, p3, p4):
    log_decay = -decay_scale * sigmoid(p0 + decay_low)
    in_rate = sigmoid(p1 + rate_low)
    value = value_raw + (first_value - value_raw) * sigmoid(p2 + value_low)
    key_norm = key_raw * p3
    key_norm = key_norm * lax.rsqrt(head_sums(key_norm * key_norm) + key_eps)
    key_used = key_raw * (1.0 + (in_rate - 1.0) * p4)
    return log_decay, key_norm, key_norm * in_rate, value, key_used


def mixer_output(state_out, receptance, key_used, value, gate, p5, p6, p7):
    center = head_sums(state_out) * (1.0 / HEAD)
    moved = state_out - center
    spread = head_sums(moved * moved) * (1.0 / HEAD)
    standard = moved * lax.rsqrt(spread + gn_eps)
    bonus = head_sums(receptance * key_used * p5) * value
    return (standard * p6 + p7 + bonus) * gate


def ordered_sums(values, reverse):
    tokens = values.shape[0]
    rows = lax.broadcasted_iota(jnp.int32, (tokens, tokens), 0)
    cols = lax.broadcasted_iota(jnp.int32, (tokens, tokens), 1)
    keep = ((cols >= rows) if reverse else (cols <= rows)).astype(jnp.bfloat16)
    total = None
    left = values
    for _ in range(3):
        part = left.astype(jnp.bfloat16)
        left = left - part.astype(jnp.float32)
        term = jnp.dot(keep, part, preferred_element_type=jnp.float32)
        total = term if total is None else total + term
    return total


def token_masks(doc_col, doc_row):
    tokens = doc_col.shape[0]
    rows = lax.broadcasted_iota(jnp.int32, (tokens, tokens), 0)
    cols = lax.broadcasted_iota(jnp.int32, (tokens, tokens), 1)
    same = doc_col == doc_row
    return same & (cols < rows), same & (cols <= rows), rows, cols


def scaled_factors(receptance, log_decay, key_norm, rate_key, key_used):
    tokens = receptance.shape[0]
    total = ordered_sums(log_decay, False)
    total = total - total[tokens // 2 - 1 : tokens // 2, :]
    up = jnp.exp(total)
    up_before = jnp.exp(total - log_decay)
    down = jnp.exp(-total)
    return up, up_before, down


def pair_products(left_factors, right_factors, strict, inclusive):
    tokens = strict.shape[0]
    left_high, left_low = split_two(left_factors)
    right_high, right_low = split_two(right_factors)
    left = jnp.concatenate([left_high, left_high, left_low], axis=1)
    right = jnp.concatenate([right_high, right_low, right_high], axis=1)
    gram = lax.dot_general(left, right, dims(1, 1), preferred_element_type=jnp.float32)
    return (
        jnp.where(strict, gram[:tokens, :tokens], 0.0),
        jnp.where(strict, gram[:tokens, tokens:], 0.0),
        jnp.where(inclusive, gram[tokens:, :tokens], 0.0),
        jnp.where(inclusive, gram[tokens:, tokens:], 0.0),
    )


def unit_inverse(lower, rows, cols):
    tokens = lower.shape[0]
    inverse = jnp.where(
        rows == cols, 1.0, jnp.where((rows // 2) == (cols // 2), lower, 0.0)
    )
    size = 2
    while size < tokens:
        inside = ((rows // (2 * size)) == (cols // (2 * size))) & ((rows // size) != (cols // size))
        border = split_two(jnp.where(inside, lower, 0.0))
        parts = split_two(inverse)
        step = dot_fine(border, parts, dims(1, 0))
        inverse = inverse + dot_fine(parts, split_two(step), dims(1, 0))
        size *= 2
    return inverse


def forward_kernel(
    rec_ref, key_ref, val_ref, first_ref, dl_ref, rl_ref, vl_ref, gate_ref, par_ref, dc_ref, dr_ref,
    core_ref, state_ref, solved_ref, inverse_ref,
):
    p = [par_ref[i : i + 1, :] for i in range(8)]
    receptance = rec_ref[...]
    log_decay, key_norm, rate_key, value, key_used = mixer_inputs(
        key_ref[...], val_ref[...], first_ref[...], dl_ref[...], rl_ref[...], vl_ref[...], *p[:5]
    )
    strict, inclusive, rows, cols = token_masks(dc_ref[...], dr_ref[...])
    up, up_before, down = scaled_factors(receptance, log_decay, key_norm, rate_key, key_used)
    a_all, r_all = -key_norm * up_before, receptance * up
    b_all, k_all = rate_key * down, key_used * down
    heads = receptance.shape[1] // HEAD
    outs, solves = [], []
    for h in range(heads):
        span = slice(h * HEAD, (h + 1) * HEAD)
        m_ab, m_ak, m_rb, m_rk = pair_products(
            jnp.concatenate([a_all[:, span], r_all[:, span]], axis=0),
            jnp.concatenate([b_all[:, span], k_all[:, span]], axis=0),
            strict,
            inclusive,
        )
        inverse = unit_inverse(m_ab, rows, cols)
        inverse_ref[h] = inverse
        v_parts = split_two(value[:, span])
        carried = dot_fine(split_two(m_ak), v_parts, dims(1, 0))
        solved = dot_fine(split_two(inverse), split_two(carried), dims(1, 0))
        outs.append(
            dot_fine(split_two(m_rb), split_two(solved), dims(1, 0))
            + dot_fine(split_two(m_rk), v_parts, dims(1, 0))
        )
        solves.append(solved)
    state_out = jnp.concatenate(outs, axis=1)
    state_ref[...] = state_out
    solved_ref[...] = jnp.concatenate(solves, axis=1)
    core_ref[...] = mixer_output(
        state_out, receptance, key_used, value, gate_ref[...], *p[5:]
    ).astype(core_ref.dtype)


def backward_kernel(
    rec_ref, key_ref, val_ref, first_ref, dl_ref, rl_ref, vl_ref, gate_ref, par_ref, dc_ref, dr_ref,
    state_ref, solved_ref, inverse_ref, grad_ref,
    d_rkv_ref, d_first_ref, d_low_ref, d_par_ref,
):
    p = [par_ref[i : i + 1, :] for i in range(8)]
    receptance = rec_ref[...]
    (log_decay, key_norm, rate_key, value, key_used), inputs_back = jax.vjp(
        mixer_inputs,
        key_ref[...], val_ref[...], first_ref[...], dl_ref[...], rl_ref[...], vl_ref[...], *p[:5]
    )
    state_out = state_ref[...]
    _, output_back = jax.vjp(
        mixer_output, state_out, receptance, key_used, value, gate_ref[...], *p[5:]
    )
    d_state, d_rec, d_key_used, d_value, d_gate, g5, g6, g7 = output_back(grad_ref[...])
    strict, inclusive, rows, cols = token_masks(dc_ref[...], dr_ref[...])
    up, up_before, down = scaled_factors(receptance, log_decay, key_norm, rate_key, key_used)
    a_all, r_all = -key_norm * up_before, receptance * up
    b_all, k_all = rate_key * down, key_used * down
    solved_all = solved_ref[...]
    tokens = receptance.shape[0]
    heads = receptance.shape[1] // HEAD
    d_a, d_r, d_b, d_k, d_v = [], [], [], [], []
    for h in range(heads):
        span = slice(h * HEAD, (h + 1) * HEAD)
        left_factors = jnp.concatenate([a_all[:, span], r_all[:, span]], axis=0)
        right_factors = jnp.concatenate([b_all[:, span], k_all[:, span]], axis=0)
        m_ab, m_ak, m_rb, m_rk = pair_products(left_factors, right_factors, strict, inclusive)
        d_out = d_state[:, span]
        d_out_parts = split_two(d_out)
        d_solved = dot_fine(split_two(m_rb), d_out_parts, dims(0, 0))
        d_carried = dot_fine(split_two(inverse_ref[h]), split_two(d_solved), dims(0, 0))
        d_carried_parts = split_two(d_carried)
        d_v.append(
            dot_fine(split_two(m_ak), d_carried_parts, dims(0, 0))
            + dot_fine(split_two(m_rk), d_out_parts, dims(0, 0))
        )
        outer_left = split_two(jnp.concatenate([d_carried, d_out], axis=0))
        outer_right = split_two(jnp.concatenate([solved_all[:, span], value[:, span]], axis=0))
        d_gram = dot_fine(outer_left, outer_right, dims(1, 1))
        both = lambda mask: jnp.concatenate([mask, mask], axis=1)
        d_gram = jnp.concatenate(
            [
                jnp.concatenate(
                    [
                        jnp.where(strict, d_gram[:tokens, :tokens], 0.0),
                        jnp.where(strict, d_gram[:tokens, tokens:], 0.0),
                    ],
                    axis=1,
                ),
                jnp.concatenate(
                    [
                        jnp.where(inclusive, d_gram[tokens:, :tokens], 0.0),
                        jnp.where(inclusive, d_gram[tokens:, tokens:], 0.0),
                    ],
                    axis=1,
                ),
            ],
            axis=0,
        )
        d_gram_parts = split_two(d_gram)
        d_left = dot_fine(d_gram_parts, split_two(right_factors), dims(1, 0))
        d_right = dot_fine(d_gram_parts, split_two(left_factors), dims(0, 0))
        d_a.append(d_left[:tokens])
        d_r.append(d_left[tokens:])
        d_b.append(d_right[:tokens])
        d_k.append(d_right[tokens:])
    d_a, d_r, d_b, d_k, d_v = [jnp.concatenate(x, axis=1) for x in (d_a, d_r, d_b, d_k, d_v)]
    before = d_a * a_all
    d_total = before + d_r * r_all - d_b * b_all - d_k * k_all
    d_log_decay = ordered_sums(d_total, True) - before
    d_rec = d_rec + d_r * up
    d_key_norm = -(d_a * up_before)
    d_rate_key = d_b * down
    d_key_used = d_key_used + d_k * down
    d_value = d_value + d_v
    d_key, d_val, d_first, d_dl, d_rl, d_vl, g0, g1, g2, g3, g4 = inputs_back(
        (d_log_decay, d_key_norm, d_rate_key, d_value, d_key_used)
    )
    d_first_ref[...] = d_first
    for i, part in enumerate((d_rec, d_key, d_val)):
        d_rkv_ref[i] = part.astype(d_rkv_ref.dtype)
    for i, part in enumerate((d_dl, d_rl, d_vl, d_gate)):
        d_low_ref[i] = part.astype(d_low_ref.dtype)
    for i, part in enumerate((g0, g1, g2, g3, g4, g5, g6, g7)):
        d_par_ref[i : i + 1, :] = part


def mix_forward(*inputs):
    tokens, width = inputs[0].shape
    full = jax.ShapeDtypeStruct((tokens, width), jnp.float32)
    return pl.pallas_call(
        forward_kernel,
        name="mix_forward",
        out_shape=(
            jax.ShapeDtypeStruct((tokens, width), jnp.bfloat16),
            full,
            full,
            jax.ShapeDtypeStruct((width // HEAD, tokens, tokens), jnp.float32),
        ),
        compiler_params=pltpu.CompilerParams(vmem_limit_bytes=48 << 20),
        interpret=interpreted,
    )(*inputs)


def mix_backward(*inputs):
    tokens, width = inputs[0].shape
    return pl.pallas_call(
        backward_kernel,
        name="mix_backward",
        out_shape=(
            jax.ShapeDtypeStruct((3, tokens, width), jnp.bfloat16),
            jax.ShapeDtypeStruct((tokens, width), jnp.float32),
            jax.ShapeDtypeStruct((4, tokens, width), jnp.bfloat16),
            jax.ShapeDtypeStruct((8, width), jnp.float32),
        ),
        compiler_params=pltpu.CompilerParams(vmem_limit_bytes=48 << 20),
        interpret=interpreted,
    )(*inputs)


def plain_timing(left, right):
    return jnp.dot(left, right, preferred_element_type=jnp.float32)


def backward_timing(left, right):
    return lax.dot_general(
        left, right, (((1,), (1,)), ((), ())), preferred_element_type=jnp.float32
    )


def outer_timing(left, right):
    return lax.dot_general(
        left, right, (((0,), (0,)), ((), ())), preferred_element_type=jnp.float32
    )


def grid_totals(values):
    return lax.psum(values.astype(jnp.bfloat16), ("row", "col")).astype(jnp.float32)


def gather_cols(values):
    return lax.all_gather(values, "col", axis=2, tiled=True)


def gather_rows(values):
    return lax.all_gather(values, "row", axis=2, tiled=True)


def reduce_rows(values):
    return lax.psum_scatter(
        values.astype(jnp.bfloat16), "row", scatter_dimension=2, tiled=True
    ).astype(jnp.float32)


def reduce_cols(values):
    return lax.psum_scatter(
        values.astype(jnp.bfloat16), "col", scatter_dimension=2, tiled=True
    ).astype(jnp.float32)


def norm_forward(values, gain, bias):
    totals = (
        grid_totals(jnp.stack([jnp.sum(values, axis=1), jnp.sum(values * values, axis=1)], axis=1))
        / EMBED_SIZE
    )
    center = totals[:, 0:1]
    inv_std = lax.rsqrt(totals[:, 1:2] - center * center + ln_eps)
    scaled = (values - center) * inv_std
    return (scaled * gain + bias, scaled, inv_std)


def norm_backward(grad_out, scaled, inv_std, gain):
    grad_scaled = grad_out * gain
    totals = (
        grid_totals(
            jnp.stack([jnp.sum(grad_scaled, axis=1), jnp.sum(grad_scaled * scaled, axis=1)], axis=1)
        )
        / EMBED_SIZE
    )
    return (grad_scaled - totals[:, 0:1] - scaled * totals[:, 1:2]) * inv_std


def shift_prev(values, same_doc):
    moved = jnp.concatenate([jnp.zeros_like(values[:1]), values[:-1]], axis=0)
    return moved * same_doc[:, None]


def shift_next(values, same_doc):
    weighted = values * same_doc[:, None]
    return jnp.concatenate([weighted[1:], jnp.zeros_like(values[:1])], axis=0)


def local(
    layer_input_rows,
    first_layer_values,
    document_index,
    output_cotangent,
    feature_parameters,
    head_parameters,
    receptance_weight,
    key_weight,
    value_weight,
    output_weight,
    channel_key_weight,
    channel_value_weight,
    down_factors,
    up_factors,
):
    same_doc = jnp.concatenate(
        [
            jnp.zeros((1,), jnp.float32),
            (document_index[0, 1:] == document_index[0, :-1]).astype(jnp.float32),
        ]
    )
    normed_one, scaled_one, inv_one = norm_forward(
        layer_input_rows, feature_parameters[0], feature_parameters[1]
    )
    delta_one = shift_prev(normed_one, same_doc) - normed_one
    time_mixes = feature_parameters[4:10]
    mixed_all = (normed_one[None] + delta_one[None] * time_mixes[:, None, :]).astype(jnp.bfloat16)
    proj_weights = (receptance_weight, key_weight, value_weight)
    proj_blocks = gather_cols(mixed_all[0:3])
    partial_proj = jnp.stack(
        [
            plain_timing(proj_blocks[position_index], proj_weights[position_index])
            for position_index in range(3)
        ],
        axis=0,
    )
    projected = reduce_rows(partial_proj)
    border_first = LOWRANK_DECAY
    border_second = border_first + LOWRANK_RATE
    border_third = border_second + LOWRANK_VALUE
    border_fourth = border_third + LOWRANK_GATE
    segment_bounds = (
        (0, border_first),
        (border_first, border_second),
        (border_second, border_third),
        (border_third, border_fourth),
    )
    lowrank_inputs = (mixed_all[3], mixed_all[4], mixed_all[2], mixed_all[5])
    hidden_activation = grid_totals(
        jnp.concatenate(
            [
                plain_timing(
                    lowrank_inputs[position_index],
                    down_factors[
                        :, segment_bounds[position_index][0] : segment_bounds[position_index][1]
                    ],
                )
                for position_index in range(4)
            ],
            axis=1,
        )
    )
    pieces = [
        hidden_activation[:, segment_bounds[position_index][0] : segment_bounds[position_index][1]]
        for position_index in range(4)
    ]
    acts_full = [jnp.tanh(pieces[0]), pieces[1], pieces[2], jax.nn.sigmoid(pieces[3])]
    layer_activations = [piece.astype(jnp.bfloat16) for piece in acts_full]
    lowrank_outputs = [
        plain_timing(
            layer_activations[position_index],
            up_factors[segment_bounds[position_index][0] : segment_bounds[position_index][1]],
        )
        for position_index in range(4)
    ]

    document_marks = document_index[0].astype(jnp.float32)
    mixer_args = (
        projected[0],
        projected[1],
        projected[2],
        first_layer_values,
        *lowrank_outputs,
        head_parameters,
        document_marks[:, None],
        document_marks[None, :],
    )
    core, *mixer_saved = mix_forward(*mixer_args)
    core_blocks = gather_rows(core[None])[0]
    residual_one = layer_input_rows + reduce_cols(plain_timing(core_blocks, output_weight)[None])[0]
    normed_two, scaled_two, inv_two = norm_forward(
        residual_one, feature_parameters[2], feature_parameters[3]
    )
    delta_two = shift_prev(normed_two, same_doc) - normed_two
    ffn_input = (normed_two + delta_two * feature_parameters[10]).astype(jnp.bfloat16)
    ffn_blocks = gather_cols(ffn_input[None])[0]
    pre_act = reduce_rows(plain_timing(ffn_blocks, channel_key_weight)[None])[0]
    hidden_act = jnp.square(jax.nn.relu(pre_act)).astype(jnp.bfloat16)
    hidden_blocks = gather_rows(hidden_act[None])[0]
    block_out = (
        residual_one + reduce_cols(plain_timing(hidden_blocks, channel_value_weight)[None])[0]
    )
    grad_blocks = gather_cols(output_cotangent.astype(jnp.bfloat16)[None])[0]
    channel_value_gradient = outer_timing(hidden_blocks, grad_blocks)
    grad_hidden = reduce_rows(backward_timing(grad_blocks, channel_value_weight)[None])[0]
    grad_pre = (2.0 * grad_hidden * jax.nn.relu(pre_act)).astype(jnp.bfloat16)
    pre_blocks = gather_rows(grad_pre[None])[0]
    channel_key_gradient = outer_timing(ffn_blocks, pre_blocks)
    grad_ffn_in = reduce_cols(backward_timing(pre_blocks, channel_key_weight)[None])[0]
    grad_mix_ffn = jnp.sum(grad_ffn_in * delta_two, axis=0)
    grad_normed_two = grad_ffn_in * (1.0 - feature_parameters[10]) + shift_next(
        grad_ffn_in * feature_parameters[10], same_doc
    )
    grad_gain_two = jnp.sum(grad_normed_two * scaled_two, axis=0)
    grad_bias_two = jnp.sum(grad_normed_two, axis=0)
    grad_residual = output_cotangent + norm_backward(
        grad_normed_two, scaled_two, inv_two, feature_parameters[2]
    )
    residual_blocks = gather_cols(grad_residual.astype(jnp.bfloat16)[None])[0]
    output_weight_gradient = outer_timing(core_blocks, residual_blocks)
    grad_core = reduce_rows(backward_timing(residual_blocks, output_weight)[None])[0]
    rkv_half, value_first_grad, lowrank_halfway, head_parameter_gradient = mix_backward(
        *mixer_args, *mixer_saved, grad_core
    )
    up_factor_gradient = jnp.concatenate(
        [
            outer_timing(layer_activations[position_index], lowrank_halfway[position_index])
            for position_index in range(4)
        ],
        axis=0,
    )
    grad_low_all = grid_totals(
        jnp.concatenate(
            [
                backward_timing(
                    lowrank_halfway[position_index],
                    up_factors[
                        segment_bounds[position_index][0] : segment_bounds[position_index][1]
                    ],
                )
                for position_index in range(4)
            ],
            axis=1,
        )
    )
    lowrank_hidden_gradient = [
        grad_low_all[:, segment_bounds[position_index][0] : segment_bounds[position_index][1]]
        for position_index in range(4)
    ]
    lowrank_hidden_gradient[0] = lowrank_hidden_gradient[0] * (1.0 - acts_full[0] * acts_full[0])
    lowrank_hidden_gradient[3] = lowrank_hidden_gradient[3] * acts_full[3] * (1.0 - acts_full[3])
    hidden_halfway = [piece.astype(jnp.bfloat16) for piece in lowrank_hidden_gradient]
    down_factor_gradient = jnp.concatenate(
        [
            outer_timing(lowrank_inputs[position_index], hidden_halfway[position_index])
            for position_index in range(4)
        ],
        axis=1,
    )
    lowrank_input_gradient = [
        backward_timing(
            hidden_halfway[position_index],
            down_factors[:, segment_bounds[position_index][0] : segment_bounds[position_index][1]],
        )
        for position_index in range(4)
    ]
    rkv_blocks = gather_rows(rkv_half)
    projection_gradient = [
        outer_timing(proj_blocks[position_index], rkv_blocks[position_index])
        for position_index in range(3)
    ]
    grad_proj_in = reduce_cols(
        jnp.stack(
            [
                backward_timing(rkv_blocks[position_index], proj_weights[position_index])
                for position_index in range(3)
            ],
            axis=0,
        )
    )
    grad_mixed = jnp.stack(
        [
            grad_proj_in[0],
            grad_proj_in[1],
            grad_proj_in[2] + lowrank_input_gradient[2],
            lowrank_input_gradient[0],
            lowrank_input_gradient[1],
            lowrank_input_gradient[3],
        ],
        axis=0,
    )
    grad_mixes = jnp.sum(grad_mixed * delta_one[None], axis=1)
    grad_normed_one = jnp.sum(grad_mixed * (1.0 - time_mixes[:, None, :]), axis=0) + shift_next(
        jnp.sum(grad_mixed * time_mixes[:, None, :], axis=0), same_doc
    )
    grad_gain_one = jnp.sum(grad_normed_one * scaled_one, axis=0)
    grad_bias_one = jnp.sum(grad_normed_one, axis=0)
    input_grad = grad_residual + norm_backward(
        grad_normed_one, scaled_one, inv_one, feature_parameters[0]
    )
    feature_gradient = jnp.concatenate(
        [
            jnp.stack([grad_gain_one, grad_bias_one, grad_gain_two, grad_bias_two]),
            grad_mixes,
            grad_mix_ffn[None],
        ],
        axis=0,
    )
    (
        feature_gradient,
        head_parameter_gradient,
        grad_recep,
        grad_key,
        grad_value,
        output_weight_gradient,
        channel_key_gradient,
        channel_value_gradient,
        down_factor_gradient,
        up_factor_gradient,
    ) = (
        lax.psum(feature_gradient.astype(jnp.bfloat16), "dp").astype(jnp.float32),
        lax.psum(head_parameter_gradient.astype(jnp.bfloat16), "dp").astype(jnp.float32),
        lax.psum(projection_gradient[0].astype(jnp.bfloat16), "dp").astype(jnp.float32),
        lax.psum(projection_gradient[1].astype(jnp.bfloat16), "dp").astype(jnp.float32),
        lax.psum(projection_gradient[2].astype(jnp.bfloat16), "dp").astype(jnp.float32),
        lax.psum(output_weight_gradient.astype(jnp.bfloat16), "dp").astype(jnp.float32),
        lax.psum(channel_key_gradient.astype(jnp.bfloat16), "dp").astype(jnp.float32),
        lax.psum(channel_value_gradient.astype(jnp.bfloat16), "dp").astype(jnp.float32),
        lax.psum(down_factor_gradient.astype(jnp.bfloat16), "dp").astype(jnp.float32),
        lax.psum(up_factor_gradient.astype(jnp.bfloat16), "dp").astype(jnp.float32),
    )
    return (
        block_out,
        input_grad,
        value_first_grad,
        feature_gradient,
        head_parameter_gradient,
        grad_recep,
        grad_key,
        grad_value,
        output_weight_gradient,
        channel_key_gradient,
        channel_value_gradient,
        down_factor_gradient,
        up_factor_gradient,
    )


def solution(mesh):
    placed = (
        P("dp", ("row", "col")),
        P("dp", ("col", "row")),
        P("dp", None),
        P("dp", ("row", "col")),
        P(None, ("row", "col")),
        P(None, ("col", "row")),
        P("row", "col"),
        P("row", "col"),
        P("row", "col"),
        P("col", "row"),
        P("row", "col"),
        P("col", "row"),
        P(("row", "col"), None),
        P(None, ("col", "row")),
    )
    return jax.shard_map(
        local,
        mesh=mesh,
        in_specs=placed,
        out_specs=(
            P("dp", ("row", "col")),
            P("dp", ("row", "col")),
            P("dp", ("col", "row")),
            P(None, ("row", "col")),
            P(None, ("col", "row")),
            P("row", "col"),
            P("row", "col"),
            P("row", "col"),
            P("col", "row"),
            P("row", "col"),
            P("col", "row"),
            P(("row", "col"), None),
            P(None, ("col", "row")),
        ),
        check_vma=False,
    )
```

```python
import jax
import jax.numpy as jnp
from jax import lax
from jax.experimental import pallas as pl
from jax.experimental.pallas import tpu as pltpu
from jax.sharding import PartitionSpec as P

EMBED_SIZE = 1024
LOWRANK_DECAY = 64
LOWRANK_RATE = 64
LOWRANK_VALUE = 32
LOWRANK_GATE = 160
ln_eps = 1e-05
HEAD = 64
gn_eps = 1.0
key_eps = 1e-06
decay_scale = 0.6065306597126334
interpreted = False


def split_two(values):
    high = values.astype(jnp.bfloat16)
    return high, (values - high.astype(jnp.float32)).astype(jnp.bfloat16)


def dims(left, right):
    return (((left,), (right,)), ((), ()))


def dot_fine(left, right, numbers):
    left_high, left_low = left
    right_high, right_low = right

    def one(a, b):
        return lax.dot_general(a, b, numbers, preferred_element_type=jnp.float32)

    return one(left_high, right_high) + (one(left_high, right_low) + one(left_low, right_high))


def head_ones(width):
    rows = lax.broadcasted_iota(jnp.int32, (width, width), 0) // HEAD
    cols = lax.broadcasted_iota(jnp.int32, (width, width), 1) // HEAD
    return (rows == cols).astype(jnp.bfloat16)


def raw_head_sums(values):
    ones = head_ones(values.shape[1])
    high, low = split_two(values)
    numbers = dims(1, 0)
    return lax.dot_general(
        high, ones, numbers, preferred_element_type=jnp.float32
    ) + lax.dot_general(low, ones, numbers, preferred_element_type=jnp.float32)


@jax.custom_vjp
def head_sums(values):
    return raw_head_sums(values)


head_sums.defvjp(lambda values: (raw_head_sums(values), None), lambda _, grad: (raw_head_sums(grad),))


def sigmoid(values):
    return 1.0 / (1.0 + jnp.exp(-values))


def mixer_inputs(key_raw, value_raw, first_value, decay_low, rate_low, value_low, p0, p1, p2, p3, p4):
    log_decay = -decay_scale * sigmoid(p0 + decay_low)
    in_rate = sigmoid(p1 + rate_low)
    value = value_raw + (first_value - value_raw) * sigmoid(p2 + value_low)
    key_norm = key_raw * p3
    key_norm = key_norm * lax.rsqrt(head_sums(key_norm * key_norm) + key_eps)
    key_used = key_raw * (1.0 + (in_rate - 1.0) * p4)
    return log_decay, key_norm, key_norm * in_rate, value, key_used


def mixer_output(state_out, receptance, key_used, value, gate, p5, p6, p7):
    center = head_sums(state_out) * (1.0 / HEAD)
    moved = state_out - center
    spread = head_sums(moved * moved) * (1.0 / HEAD)
    standard = moved * lax.rsqrt(spread + gn_eps)
    bonus = head_sums(receptance * key_used * p5) * value
    return (standard * p6 + p7 + bonus) * gate


def ordered_sums(values, reverse):
    tokens = values.shape[0]
    rows = lax.broadcasted_iota(jnp.int32, (tokens, tokens), 0)
    cols = lax.broadcasted_iota(jnp.int32, (tokens, tokens), 1)
    keep = ((cols >= rows) if reverse else (cols <= rows)).astype(jnp.bfloat16)
    total = None
    left = values
    for _ in range(3):
        part = left.astype(jnp.bfloat16)
        left = left - part.astype(jnp.float32)
        term = jnp.dot(keep, part, preferred_element_type=jnp.float32)
        total = term if total is None else total + term
    return total


def token_masks(doc_col, doc_row):
    tokens = doc_col.shape[0]
    rows = lax.broadcasted_iota(jnp.int32, (tokens, tokens), 0)
    cols = lax.broadcasted_iota(jnp.int32, (tokens, tokens), 1)
    same = doc_col == doc_row
    return same & (cols < rows), same & (cols <= rows), rows, cols


def scaled_factors(log_decay):
    tokens = log_decay.shape[0]
    total = ordered_sums(log_decay, False)
    total = total - total[tokens // 2 - 1 : tokens // 2, :]
    up = jnp.exp(total)
    up_before = jnp.exp(total - log_decay)
    down = jnp.exp(-total)
    return up, up_before, down


def pair_products(left_factors, right_factors, strict, inclusive):
    tokens = strict.shape[0]
    left_high, left_low = split_two(left_factors)
    right_high, right_low = split_two(right_factors)
    left = jnp.concatenate([left_high, left_high, left_low], axis=1)
    right = jnp.concatenate([right_high, right_low, right_high], axis=1)
    gram = lax.dot_general(left, right, dims(1, 1), preferred_element_type=jnp.float32)
    return (
        jnp.where(strict, gram[:tokens, :tokens], 0.0),
        jnp.where(strict, gram[:tokens, tokens:], 0.0),
        jnp.where(inclusive, gram[tokens:, :tokens], 0.0),
        jnp.where(inclusive, gram[tokens:, tokens:], 0.0),
    )


def unit_inverse(lower, rows, cols):
    tokens = lower.shape[0]
    inverse = jnp.where(
        rows == cols, 1.0, jnp.where((rows // 2) == (cols // 2), lower, 0.0)
    )
    size = 2
    while size < tokens:
        inside = ((rows // (2 * size)) == (cols // (2 * size))) & ((rows // size) != (cols // size))
        border = split_two(jnp.where(inside, lower, 0.0))
        parts = split_two(inverse)
        step = dot_fine(border, parts, dims(1, 0))
        inverse = inverse + dot_fine(parts, split_two(step), dims(1, 0))
        size *= 2
    return inverse


def state_forward(parts, p, marks_col, marks_row, solved_store, inverse_store):
    receptance, key_raw, value_raw, first_value, decay_low, rate_low, value_low, gate = parts
    log_decay, key_norm, rate_key, value, key_used = mixer_inputs(
        key_raw, value_raw, first_value, decay_low, rate_low, value_low, *p[:5]
    )
    strict, inclusive, rows, cols = token_masks(marks_col, marks_row)
    up, up_before, down = scaled_factors(log_decay)
    a_all, r_all = -key_norm * up_before, receptance * up
    b_all, k_all = rate_key * down, key_used * down
    outs, solves = [], []
    for h in range(receptance.shape[1] // HEAD):
        span = slice(h * HEAD, (h + 1) * HEAD)
        m_ab, m_ak, m_rb, m_rk = pair_products(
            jnp.concatenate([a_all[:, span], r_all[:, span]], axis=0),
            jnp.concatenate([b_all[:, span], k_all[:, span]], axis=0),
            strict,
            inclusive,
        )
        inverse = unit_inverse(m_ab, rows, cols)
        inverse_store[h] = inverse
        v_parts = split_two(value[:, span])
        carried = dot_fine(split_two(m_ak), v_parts, dims(1, 0))
        solved = dot_fine(split_two(inverse), split_two(carried), dims(1, 0))
        outs.append(
            dot_fine(split_two(m_rb), split_two(solved), dims(1, 0))
            + dot_fine(split_two(m_rk), v_parts, dims(1, 0))
        )
        solves.append(solved)
    state_out = jnp.concatenate(outs, axis=1)
    solved_store[...] = jnp.concatenate(solves, axis=1)
    return state_out, mixer_output(state_out, receptance, key_used, value, gate, *p[5:])


def state_backward(
    parts, p, marks_col, marks_row, state_out, solved_all, inverse_store, grad_core
):
    receptance, key_raw, value_raw, first_value, decay_low, rate_low, value_low, gate = parts
    (log_decay, key_norm, rate_key, value, key_used), inputs_back = jax.vjp(
        mixer_inputs,
        key_raw, value_raw, first_value, decay_low, rate_low, value_low, *p[:5]
    )
    _, output_back = jax.vjp(
        mixer_output, state_out, receptance, key_used, value, gate, *p[5:]
    )
    d_state, d_rec, d_key_used, d_value, d_gate, g5, g6, g7 = output_back(grad_core)
    strict, inclusive, _, _ = token_masks(marks_col, marks_row)
    up, up_before, down = scaled_factors(log_decay)
    a_all, r_all = -key_norm * up_before, receptance * up
    b_all, k_all = rate_key * down, key_used * down
    tokens = receptance.shape[0]
    heads = receptance.shape[1] // HEAD
    d_a, d_r, d_b, d_k, d_v = [], [], [], [], []
    for h in range(heads):
        span = slice(h * HEAD, (h + 1) * HEAD)
        left_factors = jnp.concatenate([a_all[:, span], r_all[:, span]], axis=0)
        right_factors = jnp.concatenate([b_all[:, span], k_all[:, span]], axis=0)
        _, m_ak, m_rb, m_rk = pair_products(left_factors, right_factors, strict, inclusive)
        d_out = d_state[:, span]
        d_out_parts = split_two(d_out)
        d_solved = dot_fine(split_two(m_rb), d_out_parts, dims(0, 0))
        d_carried = dot_fine(split_two(inverse_store[h]), split_two(d_solved), dims(0, 0))
        d_carried_parts = split_two(d_carried)
        d_v.append(
            dot_fine(split_two(m_ak), d_carried_parts, dims(0, 0))
            + dot_fine(split_two(m_rk), d_out_parts, dims(0, 0))
        )
        outer_left = split_two(jnp.concatenate([d_carried, d_out], axis=0))
        outer_right = split_two(jnp.concatenate([solved_all[:, span], value[:, span]], axis=0))
        d_gram = dot_fine(outer_left, outer_right, dims(1, 1))
        d_gram = jnp.concatenate(
            [
                jnp.concatenate(
                    [
                        jnp.where(strict, d_gram[:tokens, :tokens], 0.0),
                        jnp.where(strict, d_gram[:tokens, tokens:], 0.0),
                    ],
                    axis=1,
                ),
                jnp.concatenate(
                    [
                        jnp.where(inclusive, d_gram[tokens:, :tokens], 0.0),
                        jnp.where(inclusive, d_gram[tokens:, tokens:], 0.0),
                    ],
                    axis=1,
                ),
            ],
            axis=0,
        )
        d_gram_parts = split_two(d_gram)
        d_left = dot_fine(d_gram_parts, split_two(right_factors), dims(1, 0))
        d_right = dot_fine(d_gram_parts, split_two(left_factors), dims(0, 0))
        d_a.append(d_left[:tokens])
        d_r.append(d_left[tokens:])
        d_b.append(d_right[:tokens])
        d_k.append(d_right[tokens:])
    d_a, d_r, d_b, d_k, d_v = [jnp.concatenate(x, axis=1) for x in (d_a, d_r, d_b, d_k, d_v)]
    before = d_a * a_all
    d_total = before + d_r * r_all - d_b * b_all - d_k * k_all
    d_log_decay = ordered_sums(d_total, True) - before
    d_rec = d_rec + d_r * up
    d_key_norm = -(d_a * up_before)
    d_rate_key = d_b * down
    d_key_used = d_key_used + d_k * down
    d_value = d_value + d_v
    d_key, d_val, d_first, d_dl, d_rl, d_vl, g0, g1, g2, g3, g4 = inputs_back(
        (d_log_decay, d_key_norm, d_rate_key, d_value, d_key_used)
    )
    return (
        (d_rec, d_key, d_val),
        d_first,
        (d_dl, d_rl, d_vl, d_gate),
        (g0, g1, g2, g3, g4, g5, g6, g7),
    )


group = ("row", "col")
low_sizes = (LOWRANK_DECAY, LOWRANK_RATE, LOWRANK_VALUE, LOWRANK_GATE)
low_total = sum(low_sizes)
low_edges = (
    (0, LOWRANK_DECAY),
    (LOWRANK_DECAY, LOWRANK_DECAY + LOWRANK_RATE),
    (LOWRANK_DECAY + LOWRANK_RATE, LOWRANK_DECAY + LOWRANK_RATE + LOWRANK_VALUE),
    (LOWRANK_DECAY + LOWRANK_RATE + LOWRANK_VALUE, low_total),
)
low_streams = (3, 4, 2, 5)
pad_rows = 16
pack_tokens = 256
piece_offsets = (0, 2, 4, 6, 1, 3, 5, 7)


def plain_dot(left, right):
    return lax.dot_general(left, right, dims(1, 0), preferred_element_type=jnp.float32)


def backward_dot(left, right):
    return lax.dot_general(left, right, dims(1, 1), preferred_element_type=jnp.float32)


def outer_dot(left, right):
    return lax.dot_general(left, right, dims(0, 0), preferred_element_type=jnp.float32)


def half(values):
    return values.astype(jnp.bfloat16)


def single(values):
    return values.astype(jnp.float32)


def prev_rows(values, keep):
    return pltpu.roll(values, 1, 0) * keep


def next_rows(values, keep):
    return pltpu.roll(values * keep, values.shape[0] - 1, 0)


def joined(ref, rows):
    return jnp.concatenate([ref[i, rows, :] for i in range(ref.shape[0])], axis=1)


def token_stats(values):
    center = jnp.sum(values, axis=1, keepdims=True) * (1.0 / EMBED_SIZE)
    squares = jnp.sum(values * values, axis=1, keepdims=True) * (1.0 / EMBED_SIZE)
    return center, lax.rsqrt(squares - center * center + ln_eps)


def rows_block(rows, width):
    index = lax.broadcasted_iota(jnp.int32, (pad_rows, width), 0)
    block = jnp.zeros((pad_rows, width), jnp.float32)
    for i, row in enumerate(rows):
        block = jnp.where(index == i, row, block)
    return block


def column_as_rows(column, width):
    tokens = column.shape[0]
    turned = jnp.transpose(jnp.broadcast_to(column, (tokens, width)))
    return [turned[:pad_rows, i : i + width] for i in range(0, tokens, width)]


def rows_as_column(rows):
    width = rows[0].shape[1]
    return jnp.concatenate(
        [jnp.transpose(jnp.broadcast_to(row, (width, width))) for row in rows], axis=0
    )


def token_marks(doc_ref):
    row = single(doc_ref[...])
    tokens = row.shape[1]
    column = jnp.transpose(jnp.broadcast_to(row, (128, tokens)))
    index = lax.broadcasted_iota(jnp.int32, column.shape, 0)
    keep = jnp.where((pltpu.roll(column, 1, 0) == column) & (index > 0), 1.0, 0.0)
    return column[:, :1], row, keep[:, :1]


def pack_inputs(
    place_ref, input_ref, feat_ref, down_ref, cot_ref, rec_ref, key_ref, val_ref, chan_ref,
    packed_ref, cot_half_ref, proj_ref, proj_away_ref, chan_own_ref, chan_away_ref,
):
    tokens, width = input_ref.shape
    row = place_ref[0]
    packed_ref[:tokens, :] = half(input_ref[...])
    left = jnp.concatenate(
        [feat_ref[...], jnp.zeros((pad_rows - feat_ref.shape[0], width), jnp.float32)], axis=0
    )
    for i in range(3):
        part = half(left)
        packed_ref[tokens + i * pad_rows : tokens + (i + 1) * pad_rows, :] = part
        left = left - single(part)
    packed_ref[tokens + 3 * pad_rows :, :] = half(jnp.transpose(single(down_ref[...])))
    cot_half_ref[...] = half(cot_ref[...])
    for j, ref in enumerate((rec_ref, key_ref, val_ref)):
        proj_ref[j] = ref[:, pl.ds(pl.multiple_of(row * width, width), width)]
        proj_away_ref[j] = ref[:, pl.ds(pl.multiple_of((1 - row) * width, width), width)]
    span = chan_own_ref.shape[1]
    chan_own_ref[...] = chan_ref[:, pl.ds(pl.multiple_of(row * span, span), span)]
    chan_away_ref[...] = chan_ref[:, pl.ds(pl.multiple_of((1 - row) * span, span), span)]


def sum_devices(ref):
    total = single(ref[0])
    for i in range(1, ref.shape[0]):
        total = total + single(ref[i])
    return total


def time_forward(
    place_ref, *refs
):
    pieces, refs = refs[: len(piece_offsets)], refs[len(piece_offsets) :]
    packed_ref = refs[-1]
    for offset, ref in zip(piece_offsets, pieces):
        packed_ref[place_ref[2] ^ offset] = ref[...]
    time_forward_body(place_ref, packed_ref, *refs[:-1])


def time_forward_body(
    place_ref, packed_ref, own_ref, away_ref, up_ref, first_ref, par_ref, doc_ref,
    core_ref, state_ref, solved_ref, inverse_ref, parts_ref, mixed_ref, delta_ref, scaled_ref,
    params_ref, stats_ref, act0_ref, act1_ref, act2_ref, act3_ref, proj_ref,
):
    tokens = first_ref.shape[0]
    row = place_ref[0]
    proj_ref[row] = own_ref[...]
    proj_ref[1 - row] = away_ref[...]
    act_refs = (act0_ref, act1_ref, act2_ref, act3_ref)
    marks_col, marks_row, keep = token_marks(doc_ref)
    values = single(joined(packed_ref, slice(0, tokens)))
    extra = single(joined(packed_ref, slice(tokens, tokens + 3 * pad_rows)))
    params = extra[:pad_rows] + extra[pad_rows : 2 * pad_rows] + extra[2 * pad_rows :]
    params_ref[...] = params
    center, inv = token_stats(values)
    stats_ref[0] = jnp.broadcast_to(center, stats_ref.shape[1:])
    stats_ref[1] = jnp.broadcast_to(inv, stats_ref.shape[1:])
    scaled = (values - center) * inv
    scaled_ref[...] = scaled
    normed = scaled * params[0:1] + params[1:2]
    delta = prev_rows(normed, keep) - normed
    delta_ref[...] = half(delta)
    for j in range(6):
        mixed_ref[j] = half(normed + delta * params[4 + j : 5 + j])
    sources = proj_ref.shape[0]
    span = proj_ref.shape[2]
    for j in range(3):
        parts_ref[j] = sum(
            plain_dot(mixed_ref[j, :, s * span : (s + 1) * span], proj_ref[s, j])
            for s in range(sources)
        )
    down = joined(packed_ref, slice(tokens + 3 * pad_rows, packed_ref.shape[1]))
    for i, (low, high) in enumerate(low_edges):
        hidden = backward_dot(mixed_ref[low_streams[i]], down[low:high])
        act = jnp.tanh(hidden) if i == 0 else sigmoid(hidden) if i == 3 else hidden
        act_refs[i][...] = act
        parts_ref[3 + i] = plain_dot(half(act), up_ref[low:high, :])
    parts = (
        parts_ref[0], parts_ref[1], parts_ref[2], first_ref[...],
        parts_ref[3], parts_ref[4], parts_ref[5], parts_ref[6],
    )
    p = [par_ref[i : i + 1, :] for i in range(8)]
    state_out, core = state_forward(
        parts, p, marks_col, marks_row, solved_ref, inverse_ref
    )
    state_ref[...] = state_out
    for i in range(core_ref.shape[0]):
        core_ref[i] = half(core)


def channel_forward(
    place_ref, core_ref, out_ref, packed_ref, params_ref, doc_ref, own_ref, away_ref,
    hback_ref, hgot_ref,
    send_ref, att_ref, act_ref, pre_ref, stats_ref,
    wide_ref, keyw_ref,
):
    tokens, width = doc_ref.shape[1], send_ref.shape[2]
    _, _, keep = token_marks(doc_ref)
    row = place_ref[0]
    span = own_ref.shape[0]
    keyw_ref[pl.ds(pl.multiple_of(row * span, span), span), :] = own_ref[...]
    keyw_ref[pl.ds(pl.multiple_of((1 - row) * span, span), span), :] = away_ref[...]
    own_lanes = pl.ds(pl.multiple_of(place_ref[2] * width, width), width)
    rows = out_ref.shape[0]
    cols = core_ref.shape[0] // rows
    core = jnp.concatenate(
        [core_ref[i * cols + j] for j in range(cols) for i in range(rows)], axis=1
    )
    attended = jnp.concatenate(
        [plain_dot(core, out_ref[i]) for i in range(out_ref.shape[0])], axis=1
    )
    wide_ref[...] = attended
    att_ref[...] = wide_ref[:, own_lanes]
    residual = single(joined(packed_ref, slice(0, tokens))) + attended
    center, inv = token_stats(residual)
    stats_ref[0] = jnp.broadcast_to(center, stats_ref.shape[1:])
    stats_ref[1] = jnp.broadcast_to(inv, stats_ref.shape[1:])
    scaled = (residual - center) * inv
    gain, bias, mix = params_ref[2:3, :], params_ref[3:4, :], params_ref[10:11, :]
    normed = scaled * gain + bias
    ffn = normed + (prev_rows(normed, keep) - normed) * mix
    wide_ref[...] = ffn
    ffn = half(ffn)
    active = jnp.maximum(plain_dot(ffn, keyw_ref[...]), 0.0)
    hidden_width = active.shape[1]
    act_ref[:, :hidden_width] = half(active * active)
    act_ref[:, hidden_width:] = half(wide_ref[:, own_lanes])
    grad_pre = half(2.0 * (hback_ref[...] + single(hgot_ref[...])) * active)
    pre_ref[...] = grad_pre
    grad_ffn = backward_dot(grad_pre, keyw_ref[...])
    gained = grad_ffn * (gain * (1.0 - mix)) + next_rows(grad_ffn * (gain * mix), keep)
    sums = column_as_rows(jnp.sum(gained, axis=1, keepdims=True), width)
    sums = sums + column_as_rows(jnp.sum(gained * scaled, axis=1, keepdims=True), width)
    block = half(rows_block(sums, width))
    for i in range(send_ref.shape[0]):
        send_ref[i, :tokens, :] = half(grad_ffn[:, i * width : (i + 1) * width])
        send_ref[i, tokens:, :] = block


def residual_backward(
    got_ref, input_ref, att_ref, stats_ref, feat_ref, doc_ref, cot_ref,
    res_ref, grad_ref, grad_half_ref, rows_ref,
):
    tokens, width = input_ref.shape
    _, _, keep = token_marks(doc_ref)
    got = sum_devices(got_ref)
    grad_ffn = got[:tokens]
    pieces = tokens // width
    means = [
        rows_as_column([got[tokens + k * pieces + i : tokens + k * pieces + i + 1] for i in range(pieces)])
        * (1.0 / EMBED_SIZE)
        for k in range(2)
    ]
    residual = input_ref[...] + att_ref[...]
    res_ref[...] = residual
    inv = stats_ref[1]
    scaled = (residual - stats_ref[0]) * inv
    gain, bias, mix = feat_ref[2:3, :], feat_ref[3:4, :], feat_ref[10:11, :]
    normed = scaled * gain + bias
    delta = prev_rows(normed, keep) - normed
    grad_normed = grad_ffn * (1.0 - mix) + next_rows(grad_ffn * mix, keep)
    rows_ref[...] = rows_block(
        [
            jnp.sum(grad_normed * scaled, axis=0, keepdims=True),
            jnp.sum(grad_normed, axis=0, keepdims=True),
            jnp.sum(grad_ffn * delta, axis=0, keepdims=True),
        ],
        width,
    )
    grad = cot_ref[...] + (grad_normed * gain - means[0] - scaled * means[1]) * inv
    grad_ref[...] = grad
    grad_half_ref[...] = half(grad)


def time_backward(
    place_ref, resg_ref, out_ref, parts_ref, first_ref, par_ref, doc_ref,
    state_ref, solved_ref, inverse_ref, mixed_ref, delta_ref, scaled_ref, params_ref,
    packed_ref, proj_ref, up_ref, act0_ref, act1_ref, act2_ref, act3_ref,
    send_ref, rkv_ref, first_grad_ref, up_grad_ref,
):
    tokens, width = first_ref.shape
    act_refs = (act0_ref, act1_ref, act2_ref, act3_ref)
    marks_col, marks_row, keep = token_marks(doc_ref)
    own_rows = pl.ds(pl.multiple_of(place_ref[3] * width, width), width)
    grads = joined(resg_ref, slice(0, tokens))
    span = out_ref.shape[2]
    grad_core = sum(
        backward_dot(grads[:, i * span : (i + 1) * span], out_ref[i, own_rows, :])
        for i in range(out_ref.shape[0])
    )
    parts = (
        parts_ref[0], parts_ref[1], parts_ref[2], first_ref[...],
        parts_ref[3], parts_ref[4], parts_ref[5], parts_ref[6],
    )
    p = [par_ref[i : i + 1, :] for i in range(8)]
    d_rkv, d_first, d_low, d_par = state_backward(
        parts, p, marks_col, marks_row, state_ref[...], solved_ref[...], inverse_ref, grad_core
    )
    first_grad_ref[...] = d_first
    rkv = [half(part) for part in d_rkv]
    for j in range(3):
        rkv_ref[j] = rkv[j]
    up_grad_ref[low_total:, :] = half(rows_block(d_par, width))
    down = joined(packed_ref, slice(tokens + 3 * pad_rows, packed_ref.shape[1]))
    low_back = []
    for i, (low, high) in enumerate(low_edges):
        low_half = half(d_low[i])
        act = act_refs[i][...]
        up_grad_ref[low:high, :] = half(outer_dot(half(act), low_half))
        back = backward_dot(low_half, up_ref[low:high, :])
        if i == 0:
            back = back * (1.0 - act * act)
        if i == 3:
            back = back * act * (1.0 - act)
        back = half(back)
        low_back.append(back)
        grad = outer_dot(back, mixed_ref[low_streams[i]])
        for q in range(send_ref.shape[0]):
            send_ref[q, tokens + low : tokens + high, :] = half(grad[:, q * width : (q + 1) * width])
    delta = single(delta_ref[...])
    stay = moved = None
    mix_rows = []
    for j in range(6):
        back = None
        if j < 3:
            back = jnp.concatenate(
                [backward_dot(rkv[j], proj_ref[s, j]) for s in range(proj_ref.shape[0])], axis=1
            )
        if j in low_streams:
            i = low_streams.index(j)
            low, high = low_edges[i]
            term = plain_dot(low_back[i], down[low:high])
            back = term if back is None else back + term
        mix_rows.append(jnp.sum(back * delta, axis=0, keepdims=True))
        shifted = back * params_ref[4 + j : 5 + j, :]
        stay = back - shifted if stay is None else stay + (back - shifted)
        moved = shifted if moved is None else moved + shifted
    grad_normed = stay + next_rows(moved, keep)
    gained = grad_normed * params_ref[0:1, :]
    sums = column_as_rows(jnp.sum(gained, axis=1, keepdims=True), width)
    sums = sums + column_as_rows(jnp.sum(gained * scaled_ref[...], axis=1, keepdims=True), width)
    for q in range(send_ref.shape[0]):
        lanes = slice(q * width, (q + 1) * width)
        send_ref[q, :tokens, :] = half(grad_normed[:, lanes])
        send_ref[q, tokens + low_total :, :] = half(
            rows_block([row[:, lanes] for row in mix_rows] + sums, width)
        )


def input_backward(
    got_ref, input_ref, stats_ref, feat_ref, grad_ref, rows_ref,
    out_ref, small_ref,
):
    tokens, width = input_ref.shape
    got = sum_devices(got_ref)
    grad_normed = got[:tokens]
    small_ref[:low_total, :] = half(got[tokens : tokens + low_total])
    tail = got[tokens + low_total :]
    pieces = tokens // width
    means = [
        rows_as_column([tail[6 + k * pieces + i : 7 + k * pieces + i] for i in range(pieces)])
        * (1.0 / EMBED_SIZE)
        for k in range(2)
    ]
    inv = stats_ref[1]
    scaled = (input_ref[...] - stats_ref[0]) * inv
    out_ref[...] = grad_ref[...] + (
        (grad_normed * feat_ref[0:1, :] - means[0] - scaled * means[1]) * inv
    )
    rows = rows_ref[...]
    small_ref[low_total:, :] = half(
        rows_block(
            [
                jnp.sum(grad_normed * scaled, axis=0, keepdims=True),
                jnp.sum(grad_normed, axis=0, keepdims=True),
                rows[0:1],
                rows[1:2],
            ]
            + [tail[j : j + 1] for j in range(6)]
            + [rows[2:3]],
            width,
        )
    )


def channel_gradients(
    place_ref, act_own_ref, act_away_ref, pre_own_ref, pre_away_ref, side0_ref, side1_ref,
    side2_ref, side3_ref, pair0_ref, pair1_ref, pair2_ref, pair3_ref,
    key_ref, value_ref,
    ffn_ref, cot_ref,
):
    row, col, pack = place_ref[0], place_ref[1], place_ref[4]
    width = side0_ref.shape[1]
    packs = max(cot_ref.shape[0] // pack_tokens, 1)
    tokens = cot_ref.shape[0] // packs
    for k, ref in enumerate((side0_ref, side1_ref, side2_ref, side3_ref)):
        ffn_ref[:, pl.ds(pl.multiple_of((col ^ k) * width, width), width)] = ref[...]
    for k, ref in enumerate((pair0_ref, pair1_ref, pair2_ref, pair3_ref)):
        lanes = pl.ds(pl.multiple_of((col ^ k) * width, width), width)
        for m in range(packs):
            rows = pl.ds(pl.multiple_of((pack ^ m) * tokens, tokens), tokens)
            cot_ref[rows, lanes] = ref[m * tokens : (m + 1) * tokens, :]
    span = pre_own_ref.shape[1]
    for where, act, pre in (
        (row, act_own_ref, pre_own_ref), (1 - row, act_away_ref, pre_away_ref)
    ):
        block = pl.ds(pl.multiple_of(where * span, span), span)
        value_ref[block, :] = outer_dot(act[...], cot_ref[...])
        key_ref[:, block] = outer_dot(ffn_ref[...], pre[...])


def widen(
    rec_ref, key_ref, val_ref, out_ref, up_ref,
    rec_out, key_out, val_out, out_out, up_out, par_out,
):
    for source, target in (
        (rec_ref, rec_out), (key_ref, key_out), (val_ref, val_out), (out_ref, out_out)
    ):
        target[...] = single(source[...])
    rows = single(up_ref[...])
    up_out[...] = rows[:low_total]
    par_out[...] = rows[low_total : low_total + par_out.shape[0]]


def call(kernel, outs, *inputs, scratch=()):
    places = [pl.BlockSpec(memory_space=pltpu.SMEM)] if inputs[0].ndim == 1 else []
    return pl.pallas_call(
        kernel,
        in_specs=places + [pl.BlockSpec(memory_space=pltpu.VMEM)] * (len(inputs) - len(places)),
        scratch_shapes=[pltpu.VMEM(shape, dtype) for shape, dtype in scratch],
        out_shape=tuple(jax.ShapeDtypeStruct(shape, dtype) for shape, dtype in outs),
        compiler_params=pltpu.CompilerParams(vmem_limit_bytes=56 << 20),
        interpret=interpreted,
    )(*inputs)


def exchange(values, axis, offset):
    size = lax.axis_size(axis)
    return lax.ppermute(values, axis, [(i, i ^ offset) for i in range(size)])


def pick(stacked, index):
    return lax.dynamic_index_in_dim(stacked, index, 0, keepdims=False)


def power_of_two(size):
    return size & (size - 1) == 0


def gather_pieces(values, axis):
    size = lax.axis_size(axis)
    if not power_of_two(size):
        arrived = lax.all_gather(values, axis)
        return [arrived[i] for i in range(size)]
    index = lax.axis_index(axis)
    pieces = [values] + [exchange(values, axis, k) for k in range(1, size)]
    ordered = []
    for source in range(size):
        chosen = pieces[0]
        for offset in range(1, size):
            chosen = jnp.where(index ^ source == offset, pieces[offset], chosen)
        ordered.append(chosen)
    return ordered


def scatter_sum(stacked, axis):
    size = lax.axis_size(axis)
    if not power_of_two(size):
        return jnp.sum(single(lax.all_to_all(half(stacked), axis, 0, 0)), axis=0)
    index = lax.axis_index(axis)
    total = pick(stacked, index)
    for k in range(1, size):
        total = total + single(exchange(half(pick(stacked, index ^ k)), axis, k))
    return total


def small_pack_sum(values):
    if lax.axis_size("dp") != 4:
        return single(lax.psum(values, "dp"))
    near, far, both = [single(exchange(values, "dp", k)) for k in (1, 2, 3)]
    return (single(values) + near) + (far + both)


def lane_chunks(values, count):
    rows, width = values.shape
    return jnp.transpose(values.reshape(rows, count, width // count), (1, 0, 2))


def layer(
    layer_input_rows,
    first_layer_values,
    document_index,
    output_cotangent,
    feature_parameters,
    head_parameters,
    receptance_weight,
    key_weight,
    value_weight,
    output_weight,
    channel_key_weight,
    channel_value_weight,
    down_factors,
    up_factors,
):
    row_count, col_count = lax.axis_size("row"), lax.axis_size("col")
    count = row_count * col_count
    row, col = lax.axis_index("row"), lax.axis_index("col")
    tokens, width = layer_input_rows.shape
    full_width = width * count
    features, heads = feature_parameters.shape[0], head_parameters.shape[0]
    row_width = width * col_count
    hidden_width = channel_key_weight.shape[1] // row_count
    few_packs = lax.axis_size("dp") == 4
    pack = lax.axis_index("dp") if few_packs else 0
    place = jnp.stack(
        [row, col, row * col_count + col, col * row_count + row, jnp.asarray(pack, row.dtype)]
    ).astype(jnp.int32)
    f32, bf16 = jnp.float32, jnp.bfloat16
    own = (tokens, width)
    wide = (tokens, full_width)

    def row_columns(values):
        return lax.dynamic_slice_in_dim(values, row * row_width, row_width, 1)

    packed, cotangent_half, proj_own, proj_send, key_own, key_send = call(
        pack_inputs,
        [
            ((tokens + 3 * pad_rows + low_total, width), bf16),
            (own, bf16),
            ((3, row_width, width), bf16),
            ((3, row_width, width), bf16),
            ((row_width, hidden_width), bf16),
            ((row_width, hidden_width), bf16),
        ],
        place, layer_input_rows, feature_parameters, down_factors, output_cotangent,
        receptance_weight, key_weight, value_weight, channel_key_weight,
    )
    proj_away = exchange(proj_send, "row", 1)
    near = [packed] + [exchange(packed, group, k) for k in piece_offsets[1:4]]
    pieces = near + [exchange(piece, group, 1) for piece in near]
    *pieces, key_send = lax.optimization_barrier((*pieces, key_send))
    output_blocks = lax.all_gather(output_weight, group, axis=0, tiled=True).reshape(
        row_count, -1, output_weight.shape[1]
    )
    key_away = exchange(key_send, "row", 1)
    grad_pieces = gather_pieces(cotangent_half, "col")
    grad_blocks = jnp.concatenate(grad_pieces, axis=1)
    hidden_back = lane_chunks(backward_dot(grad_blocks, channel_value_weight), row_count)
    back_away = exchange(half(pick(hidden_back, 1 - row)), "row", 1)
    back_own = pick(hidden_back, row)

    (
        core, state_out, solved, inverse, parts, mixed, delta_one, scaled_one, params, stats_one,
        act0, act1, act2, act3, proj_weights, packed_all,
    ) = call(
        time_forward,
        [
            ((count,) + own, bf16),
            (own, f32),
            (own, f32),
            ((width // HEAD, tokens, tokens), f32),
            ((7,) + own, f32),
            ((6,) + wide, bf16),
            (wide, bf16),
            (wide, f32),
            ((pad_rows, full_width), f32),
            ((2,) + own, f32),
        ]
        + [((tokens, size), f32) for size in low_sizes]
        + [((row_count, 3, row_width, width), bf16), ((count,) + packed.shape, bf16)],
        place, *pieces, proj_own, proj_away, up_factors, first_layer_values,
        head_parameters, document_index,
    )
    core_all = lax.all_to_all(core, group, 0, 0)
    pair_own = cotangent_half
    if few_packs:
        pair_own = jnp.concatenate(
            [cotangent_half] + [exchange(cotangent_half, "dp", k) for k in (1, 2, 3)], axis=0
        )
    pairs = [pair_own] + [exchange(pair_own, "col", k) for k in range(1, col_count)]
    send_two, attended_own, act_side, grad_pre, stats_two = call(
        channel_forward,
        [
            ((count, tokens + pad_rows, width), bf16),
            (own, f32),
            ((tokens, hidden_width + width), bf16),
            ((tokens, hidden_width), bf16),
            ((2,) + own, f32),
        ],
        place, core_all, output_blocks, packed_all, params, document_index, key_own, key_away,
        back_own, back_away,
        scratch=[(wide, f32), ((full_width, hidden_width), bf16)],
    )
    act_all, pre_all = act_side, grad_pre
    if few_packs:
        act_all = lax.all_gather(act_side, "dp", axis=0, tiled=True)
        pre_all = lax.all_gather(grad_pre, "dp", axis=0, tiled=True)
    got_two = lax.all_to_all(send_two, group, 0, 0)
    pre_away = exchange(pre_all, "row", 1)
    residual_one, grad_residual, grad_residual_half, rows_two = call(
        residual_backward,
        [(own, f32), (own, f32), (own, bf16), ((pad_rows, width), f32)],
        got_two, layer_input_rows, attended_own, stats_two, feature_parameters, document_index,
        output_cotangent,
    )
    residual_all = lax.all_gather(grad_residual_half, group, axis=0, tiled=False)
    hidden_pieces = gather_pieces(act_side[:, :hidden_width], "row")
    hidden_blocks = jnp.concatenate(hidden_pieces, axis=1)
    block_part = plain_dot(hidden_blocks, channel_value_weight)
    block_out = residual_one + scatter_sum(lane_chunks(block_part, col_count), "col")

    send_one, rkv_half, value_first_grad, up_head_gradient = call(
        time_backward,
        [
            ((count, tokens + low_total + pad_rows, width), bf16),
            ((3,) + own, bf16),
            (own, f32),
            ((low_total + pad_rows, width), bf16),
        ],
        place, residual_all, output_blocks, parts, first_layer_values, head_parameters,
        document_index, state_out, solved, inverse, mixed, delta_one, scaled_one, params,
        packed_all, proj_weights, up_factors, act0, act1, act2, act3,
    )
    rkv_pieces = gather_pieces(rkv_half, "row")
    rkv_blocks = jnp.concatenate(rkv_pieces, axis=2)
    got_one = lax.all_to_all(send_one, group, 0, 0)
    core_block = lax.dynamic_index_in_dim(
        core_all.reshape((row_count, col_count) + own), col, 1, keepdims=False
    )
    core_block = jnp.transpose(core_block, (1, 0, 2)).reshape(tokens, -1)
    residual_block = lax.dynamic_slice_in_dim(residual_all, row * col_count, col_count, 0)
    residual_block = jnp.transpose(residual_block, (1, 0, 2)).reshape(tokens, -1)
    late = (
        *[half(outer_dot(row_columns(mixed[j]), rkv_blocks[j])) for j in range(3)],
        half(outer_dot(core_block, residual_block)),
        up_head_gradient,
    )
    late = lax.psum(late, "dp")

    act_own, side_own = act_all[:, :hidden_width], act_all[:, hidden_width:]
    act_away = exchange(act_own, "row", 1)
    sides = [exchange(side_own, "col", k) for k in range(1, col_count)]
    packs_tokens = act_all.shape[0]
    channel_key_gradient, channel_value_gradient = call(
        channel_gradients,
        [(channel_key_weight.shape, f32), (channel_value_weight.shape, f32)],
        place, act_own, act_away, pre_all, pre_away, side_own, *sides, *pairs,
        scratch=[((packs_tokens, row_width), bf16), ((packs_tokens, row_width), bf16)],
    )
    if not few_packs:
        channel_key_gradient, channel_value_gradient = [
            single(lax.psum(half(piece), "dp"))
            for piece in (channel_key_gradient, channel_value_gradient)
        ]
    input_grad, small = call(
        input_backward,
        [(own, f32), ((low_total + pad_rows, width), bf16)],
        got_one, layer_input_rows, stats_one, feature_parameters, grad_residual, rows_two,
    )
    small = small_pack_sum(small)
    late = call(
        widen,
        [(piece.shape, f32) for piece in late[:4]] + [((low_total, width), f32), ((heads, width), f32)],
        *late,
    )
    return (
        block_out,
        input_grad,
        value_first_grad,
        small[low_total : low_total + features],
        late[5],
        late[0],
        late[1],
        late[2],
        late[3],
        channel_key_gradient,
        channel_value_gradient,
        small[:low_total].T,
        late[4],
    )


def solution(mesh):
    placed = (
        P("dp", ("row", "col")),
        P("dp", ("col", "row")),
        P("dp", None),
        P("dp", ("row", "col")),
        P(None, ("row", "col")),
        P(None, ("col", "row")),
        P("row", "col"),
        P("row", "col"),
        P("row", "col"),
        P("col", "row"),
        P("row", "col"),
        P("col", "row"),
        P(("row", "col"), None),
        P(None, ("col", "row")),
    )
    return jax.shard_map(
        layer,
        mesh=mesh,
        in_specs=placed,
        out_specs=(
            P("dp", ("row", "col")),
            P("dp", ("row", "col")),
            P("dp", ("col", "row")),
            P(None, ("row", "col")),
            P(None, ("col", "row")),
            P("row", "col"),
            P("row", "col"),
            P("row", "col"),
            P("col", "row"),
            P("row", "col"),
            P("col", "row"),
            P(("row", "col"), None),
            P(None, ("col", "row")),
        ),
        check_vma=False,
    )
```

```python
import jax
import jax.numpy as jnp
from jax import lax
from jax.experimental import pallas as pl
from jax.experimental.pallas import tpu as pltpu
from jax.sharding import PartitionSpec as P

EMBED_SIZE = 1024
LOWRANK_DECAY = 64
LOWRANK_RATE = 64
LOWRANK_VALUE = 32
LOWRANK_GATE = 160
ln_eps = 1e-05
HEAD = 64
gn_eps = 1.0
key_eps = 1e-06
decay_scale = 0.6065306597126334
interpreted = False


def split_two(values):
    high = values.astype(jnp.bfloat16)
    return high, (values - high.astype(jnp.float32)).astype(jnp.bfloat16)


def dims(left, right):
    return (((left,), (right,)), ((), ()))


def dot_fine(left, right, numbers):
    left_high, left_low = left
    right_high, right_low = right

    def one(a, b):
        return lax.dot_general(a, b, numbers, preferred_element_type=jnp.float32)

    return one(left_high, right_high) + (one(left_high, right_low) + one(left_low, right_high))


def head_ones(width):
    rows = lax.broadcasted_iota(jnp.int32, (width, width), 0) // HEAD
    cols = lax.broadcasted_iota(jnp.int32, (width, width), 1) // HEAD
    return (rows == cols).astype(jnp.bfloat16)


def raw_head_sums(values):
    ones = head_ones(values.shape[1])
    high, low = split_two(values)
    numbers = dims(1, 0)
    return lax.dot_general(
        high, ones, numbers, preferred_element_type=jnp.float32
    ) + lax.dot_general(low, ones, numbers, preferred_element_type=jnp.float32)


@jax.custom_vjp
def head_sums(values):
    return raw_head_sums(values)


head_sums.defvjp(lambda values: (raw_head_sums(values), None), lambda _, grad: (raw_head_sums(grad),))


def sigmoid(values):
    return 1.0 / (1.0 + jnp.exp(-values))


def mixer_inputs(key_raw, value_raw, first_value, decay_low, rate_low, value_low, p0, p1, p2, p3, p4):
    log_decay = -decay_scale * sigmoid(p0 + decay_low)
    in_rate = sigmoid(p1 + rate_low)
    value = value_raw + (first_value - value_raw) * sigmoid(p2 + value_low)
    key_norm = key_raw * p3
    key_norm = key_norm * lax.rsqrt(head_sums(key_norm * key_norm) + key_eps)
    key_used = key_raw * (1.0 + (in_rate - 1.0) * p4)
    return log_decay, key_norm, key_norm * in_rate, value, key_used


def mixer_output(state_out, receptance, key_used, value, gate, p5, p6, p7):
    center = head_sums(state_out) * (1.0 / HEAD)
    moved = state_out - center
    spread = head_sums(moved * moved) * (1.0 / HEAD)
    standard = moved * lax.rsqrt(spread + gn_eps)
    bonus = head_sums(receptance * key_used * p5) * value
    return (standard * p6 + p7 + bonus) * gate


def ordered_sums(values, reverse):
    tokens = values.shape[0]
    rows = lax.broadcasted_iota(jnp.int32, (tokens, tokens), 0)
    cols = lax.broadcasted_iota(jnp.int32, (tokens, tokens), 1)
    keep = ((cols >= rows) if reverse else (cols <= rows)).astype(jnp.bfloat16)
    total = None
    left = values
    for _ in range(3):
        part = left.astype(jnp.bfloat16)
        left = left - part.astype(jnp.float32)
        term = jnp.dot(keep, part, preferred_element_type=jnp.float32)
        total = term if total is None else total + term
    return total


def token_masks(doc_col, doc_row):
    tokens = doc_col.shape[0]
    rows = lax.broadcasted_iota(jnp.int32, (tokens, tokens), 0)
    cols = lax.broadcasted_iota(jnp.int32, (tokens, tokens), 1)
    same = doc_col == doc_row
    return same & (cols < rows), same & (cols <= rows)


def scaled_factors(log_decay):
    tokens = log_decay.shape[0]
    total = ordered_sums(log_decay, False)
    total = total - total[tokens // 2 - 1 : tokens // 2, :]
    up = jnp.exp(total)
    up_before = jnp.exp(total - log_decay)
    down = jnp.exp(-total)
    return up, up_before, down


def pair_products(left_factors, right_factors, strict, inclusive):
    tokens = strict.shape[0]
    left_high, left_low = split_two(left_factors)
    right_high, right_low = split_two(right_factors)
    left = jnp.concatenate([left_high, left_high, left_low], axis=1)
    right = jnp.concatenate([right_high, right_low, right_high], axis=1)
    gram = lax.dot_general(left, right, dims(1, 1), preferred_element_type=jnp.float32)
    return (
        jnp.where(strict, gram[:tokens, :tokens], 0.0),
        jnp.where(strict, gram[:tokens, tokens:], 0.0),
        jnp.where(inclusive, gram[tokens:, :tokens], 0.0),
        jnp.where(inclusive, gram[tokens:, tokens:], 0.0),
    )


def unit_inverse(lower):
    tokens = lower.shape[0]
    if tokens > 128:
        mid = tokens // 2
        first = unit_inverse(lower[:mid, :mid])
        last = unit_inverse(lower[mid:, mid:])
        step = dot_fine(split_two(lower[mid:, :mid]), split_two(first), dims(1, 0))
        corner = dot_fine(split_two(last), split_two(step), dims(1, 0))
        return jnp.concatenate(
            [
                jnp.concatenate([first, jnp.zeros_like(first)], axis=1),
                jnp.concatenate([corner, last], axis=1),
            ],
            axis=0,
        )
    rows = lax.broadcasted_iota(jnp.int32, (tokens, tokens), 0)
    cols = lax.broadcasted_iota(jnp.int32, (tokens, tokens), 1)
    inverse = jnp.where(
        rows == cols, 1.0, jnp.where((rows // 2) == (cols // 2), lower, 0.0)
    )
    size = 2
    while size < tokens:
        inside = ((rows // (2 * size)) == (cols // (2 * size))) & ((rows // size) != (cols // size))
        border = split_two(jnp.where(inside, lower, 0.0))
        parts = split_two(inverse)
        step = dot_fine(border, parts, dims(1, 0))
        inverse = inverse + dot_fine(parts, split_two(step), dims(1, 0))
        size *= 2
    return inverse


def state_forward(parts, p, marks_col, marks_row, solved_store, inverse_store):
    receptance, key_raw, value_raw, first_value, decay_low, rate_low, value_low, gate = parts
    log_decay, key_norm, rate_key, value, key_used = mixer_inputs(
        key_raw, value_raw, first_value, decay_low, rate_low, value_low, *p[:5]
    )
    strict, inclusive = token_masks(marks_col, marks_row)
    up, up_before, down = scaled_factors(log_decay)
    a_all, r_all = -key_norm * up_before, receptance * up
    b_all, k_all = rate_key * down, key_used * down
    outs, solves = [], []
    for h in range(receptance.shape[1] // HEAD):
        span = slice(h * HEAD, (h + 1) * HEAD)
        m_ab, m_ak, m_rb, m_rk = pair_products(
            jnp.concatenate([a_all[:, span], r_all[:, span]], axis=0),
            jnp.concatenate([b_all[:, span], k_all[:, span]], axis=0),
            strict,
            inclusive,
        )
        inverse = unit_inverse(m_ab)
        inverse_store[h] = inverse
        v_parts = split_two(value[:, span])
        carried = dot_fine(split_two(m_ak), v_parts, dims(1, 0))
        solved = dot_fine(split_two(inverse), split_two(carried), dims(1, 0))
        outs.append(
            dot_fine(split_two(m_rb), split_two(solved), dims(1, 0))
            + dot_fine(split_two(m_rk), v_parts, dims(1, 0))
        )
        solves.append(solved)
    state_out = jnp.concatenate(outs, axis=1)
    solved_store[...] = jnp.concatenate(solves, axis=1)
    return state_out, mixer_output(state_out, receptance, key_used, value, gate, *p[5:])


def state_backward(
    parts, p, marks_col, marks_row, state_out, solved_all, inverse_store, grad_core
):
    receptance, key_raw, value_raw, first_value, decay_low, rate_low, value_low, gate = parts
    (log_decay, key_norm, rate_key, value, key_used), inputs_back = jax.vjp(
        mixer_inputs,
        key_raw, value_raw, first_value, decay_low, rate_low, value_low, *p[:5]
    )
    _, output_back = jax.vjp(
        mixer_output, state_out, receptance, key_used, value, gate, *p[5:]
    )
    d_state, d_rec, d_key_used, d_value, d_gate, g5, g6, g7 = output_back(grad_core)
    strict, inclusive = token_masks(marks_col, marks_row)
    up, up_before, down = scaled_factors(log_decay)
    a_all, r_all = -key_norm * up_before, receptance * up
    b_all, k_all = rate_key * down, key_used * down
    tokens = receptance.shape[0]
    heads = receptance.shape[1] // HEAD
    d_a, d_r, d_b, d_k, d_v = [], [], [], [], []
    for h in range(heads):
        span = slice(h * HEAD, (h + 1) * HEAD)
        left_factors = jnp.concatenate([a_all[:, span], r_all[:, span]], axis=0)
        right_factors = jnp.concatenate([b_all[:, span], k_all[:, span]], axis=0)
        _, m_ak, m_rb, m_rk = pair_products(left_factors, right_factors, strict, inclusive)
        d_out = d_state[:, span]
        d_out_parts = split_two(d_out)
        d_solved = dot_fine(split_two(m_rb), d_out_parts, dims(0, 0))
        d_carried = dot_fine(split_two(inverse_store[h]), split_two(d_solved), dims(0, 0))
        d_carried_parts = split_two(d_carried)
        d_v.append(
            dot_fine(split_two(m_ak), d_carried_parts, dims(0, 0))
            + dot_fine(split_two(m_rk), d_out_parts, dims(0, 0))
        )
        outer_left = split_two(jnp.concatenate([d_carried, d_out], axis=0))
        outer_right = split_two(jnp.concatenate([solved_all[:, span], value[:, span]], axis=0))
        d_gram = dot_fine(outer_left, outer_right, dims(1, 1))
        d_gram = jnp.concatenate(
            [
                jnp.concatenate(
                    [
                        jnp.where(strict, d_gram[:tokens, :tokens], 0.0),
                        jnp.where(strict, d_gram[:tokens, tokens:], 0.0),
                    ],
                    axis=1,
                ),
                jnp.concatenate(
                    [
                        jnp.where(inclusive, d_gram[tokens:, :tokens], 0.0),
                        jnp.where(inclusive, d_gram[tokens:, tokens:], 0.0),
                    ],
                    axis=1,
                ),
            ],
            axis=0,
        )
        d_gram_parts = split_two(d_gram)
        d_left = dot_fine(d_gram_parts, split_two(right_factors), dims(1, 0))
        d_right = dot_fine(d_gram_parts, split_two(left_factors), dims(0, 0))
        d_a.append(d_left[:tokens])
        d_r.append(d_left[tokens:])
        d_b.append(d_right[:tokens])
        d_k.append(d_right[tokens:])
    d_a, d_r, d_b, d_k, d_v = [jnp.concatenate(x, axis=1) for x in (d_a, d_r, d_b, d_k, d_v)]
    before = d_a * a_all
    d_total = before + d_r * r_all - d_b * b_all - d_k * k_all
    d_log_decay = ordered_sums(d_total, True) - before
    d_rec = d_rec + d_r * up
    d_key_norm = -(d_a * up_before)
    d_rate_key = d_b * down
    d_key_used = d_key_used + d_k * down
    d_value = d_value + d_v
    d_key, d_val, d_first, d_dl, d_rl, d_vl, g0, g1, g2, g3, g4 = inputs_back(
        (d_log_decay, d_key_norm, d_rate_key, d_value, d_key_used)
    )
    return (
        (d_rec, d_key, d_val),
        d_first,
        (d_dl, d_rl, d_vl, d_gate),
        (g0, g1, g2, g3, g4, g5, g6, g7),
    )


group = ("row", "col")
low_sizes = (LOWRANK_DECAY, LOWRANK_RATE, LOWRANK_VALUE, LOWRANK_GATE)
low_total = sum(low_sizes)
low_edges = (
    (0, LOWRANK_DECAY),
    (LOWRANK_DECAY, LOWRANK_DECAY + LOWRANK_RATE),
    (LOWRANK_DECAY + LOWRANK_RATE, LOWRANK_DECAY + LOWRANK_RATE + LOWRANK_VALUE),
    (LOWRANK_DECAY + LOWRANK_RATE + LOWRANK_VALUE, low_total),
)
low_streams = (3, 4, 2, 5)
pad_rows = 16
pack_tokens = 256
piece_offsets = (0, 2, 4, 6, 1, 3, 5, 7)


def plain_dot(left, right):
    return lax.dot_general(left, right, dims(1, 0), preferred_element_type=jnp.float32)


def backward_dot(left, right):
    return lax.dot_general(left, right, dims(1, 1), preferred_element_type=jnp.float32)


def outer_dot(left, right):
    return lax.dot_general(left, right, dims(0, 0), preferred_element_type=jnp.float32)


def half(values):
    return values.astype(jnp.bfloat16)


def single(values):
    return values.astype(jnp.float32)


def prev_rows(values, keep):
    return pltpu.roll(values, 1, 0) * keep


def next_rows(values, keep):
    return pltpu.roll(values * keep, values.shape[0] - 1, 0)


def joined(ref, rows):
    return jnp.concatenate([ref[i, rows, :] for i in range(ref.shape[0])], axis=1)


def token_stats(values):
    center = jnp.sum(values, axis=1, keepdims=True) * (1.0 / EMBED_SIZE)
    squares = jnp.sum(values * values, axis=1, keepdims=True) * (1.0 / EMBED_SIZE)
    return center, lax.rsqrt(squares - center * center + ln_eps)


def rows_block(rows, width):
    index = lax.broadcasted_iota(jnp.int32, (pad_rows, width), 0)
    block = jnp.zeros((pad_rows, width), jnp.float32)
    for i, row in enumerate(rows):
        block = jnp.where(index == i, row, block)
    return block


def column_as_rows(column, width):
    tokens = column.shape[0]
    turned = jnp.transpose(jnp.broadcast_to(column, (tokens, width)))
    return [turned[:pad_rows, i : i + width] for i in range(0, tokens, width)]


def rows_as_column(rows):
    width = rows[0].shape[1]
    return jnp.concatenate(
        [jnp.transpose(jnp.broadcast_to(row, (width, width))) for row in rows], axis=0
    )


def token_marks(doc_ref):
    row = single(doc_ref[...])
    tokens = row.shape[1]
    column = jnp.transpose(jnp.broadcast_to(row, (128, tokens)))
    index = lax.broadcasted_iota(jnp.int32, column.shape, 0)
    keep = jnp.where((pltpu.roll(column, 1, 0) == column) & (index > 0), 1.0, 0.0)
    return column[:, :1], row, keep[:, :1]


def pack_inputs(
    place_ref, input_ref, feat_ref, down_ref, cot_ref, rec_ref, key_ref, val_ref, chan_ref,
    packed_ref, cot_half_ref, proj_ref, proj_away_ref, chan_own_ref, chan_away_ref,
):
    tokens, width = input_ref.shape
    row = place_ref[0]
    packed_ref[:tokens, :] = half(input_ref[...])
    left = jnp.concatenate(
        [feat_ref[...], jnp.zeros((pad_rows - feat_ref.shape[0], width), jnp.float32)], axis=0
    )
    for i in range(3):
        part = half(left)
        packed_ref[tokens + i * pad_rows : tokens + (i + 1) * pad_rows, :] = part
        left = left - single(part)
    packed_ref[tokens + 3 * pad_rows :, :] = half(jnp.transpose(single(down_ref[...])))
    cot_half_ref[...] = half(cot_ref[...])
    for j, ref in enumerate((rec_ref, key_ref, val_ref)):
        proj_ref[j] = ref[:, pl.ds(pl.multiple_of(row * width, width), width)]
        proj_away_ref[j] = ref[:, pl.ds(pl.multiple_of((1 - row) * width, width), width)]
    span = chan_own_ref.shape[1]
    chan_own_ref[...] = chan_ref[:, pl.ds(pl.multiple_of(row * span, span), span)]
    chan_away_ref[...] = chan_ref[:, pl.ds(pl.multiple_of((1 - row) * span, span), span)]


def sum_devices(ref):
    total = single(ref[0])
    for i in range(1, ref.shape[0]):
        total = total + single(ref[i])
    return total


def time_inputs(place_ref, *refs):
    pieces, refs = refs[: len(piece_offsets)], refs[len(piece_offsets) :]
    up_ref, doc_ref, *refs = refs
    *refs, packed_ref = refs
    mixed_ref, turned_ref, delta_ref, scaled_ref, params_ref, stats_ref, lows_ref, *act_refs = refs
    for offset, ref in zip(piece_offsets, pieces):
        packed_ref[place_ref[2] ^ offset] = ref[...]
    tokens = delta_ref.shape[0]
    _, _, keep = token_marks(doc_ref)
    values = single(joined(packed_ref, slice(0, tokens)))
    extra = single(joined(packed_ref, slice(tokens, tokens + 3 * pad_rows)))
    params = extra[:pad_rows] + extra[pad_rows : 2 * pad_rows] + extra[2 * pad_rows :]
    params_ref[...] = params
    center, inv = token_stats(values)
    stats_ref[0] = jnp.broadcast_to(center, stats_ref.shape[1:])
    stats_ref[1] = jnp.broadcast_to(inv, stats_ref.shape[1:])
    scaled = (values - center) * inv
    scaled_ref[...] = scaled
    normed = scaled * params[0:1] + params[1:2]
    delta = prev_rows(normed, keep) - normed
    delta_ref[...] = half(delta)
    for j in range(3):
        mixed_ref[j] = half(normed + delta * params[4 + j : 5 + j])
        turned_ref[j] = half(normed + delta * params[7 + j : 8 + j])
    down = joined(packed_ref, slice(tokens + 3 * pad_rows, packed_ref.shape[1]))
    for i, (low, high) in enumerate(low_edges):
        hidden = backward_dot(stream(mixed_ref, turned_ref, low_streams[i]), down[low:high])
        act = jnp.tanh(hidden) if i == 0 else sigmoid(hidden) if i == 3 else hidden
        act_refs[i][...] = act
        lows_ref[i] = plain_dot(half(act), up_ref[low:high, :])


def stream(mixed_ref, turned_ref, index):
    return mixed_ref[index] if index < 3 else turned_ref[index - 3]


def time_forward(
    place_ref, mixed_ref, lows_ref, own_ref, away_ref, first_ref, par_ref, doc_ref,
    core_ref, state_ref, solved_ref, inverse_ref, rkv_ref, proj_ref,
):
    row = place_ref[0]
    proj_ref[row] = own_ref[...]
    proj_ref[1 - row] = away_ref[...]
    marks_col, marks_row, _ = token_marks(doc_ref)
    sources = proj_ref.shape[0]
    span = proj_ref.shape[2]
    for j in range(3):
        rkv_ref[j] = sum(
            plain_dot(mixed_ref[j, :, s * span : (s + 1) * span], proj_ref[s, j])
            for s in range(sources)
        )
    parts = (
        rkv_ref[0], rkv_ref[1], rkv_ref[2], first_ref[...],
        lows_ref[0], lows_ref[1], lows_ref[2], lows_ref[3],
    )
    p = [par_ref[i : i + 1, :] for i in range(8)]
    state_out, core = state_forward(parts, p, marks_col, marks_row, solved_ref, inverse_ref)
    state_ref[...] = state_out
    for i in range(core_ref.shape[0]):
        core_ref[i] = half(core)


def channel_forward(
    place_ref, core_ref, out_ref, packed_ref, params_ref, doc_ref, own_ref, away_ref,
    hback_ref, hgot_ref,
    send_ref, att_ref, act_ref, pre_ref, stats_ref,
    wide_ref, keyw_ref,
):
    tokens, width = doc_ref.shape[1], send_ref.shape[2]
    _, _, keep = token_marks(doc_ref)
    row = place_ref[0]
    span = own_ref.shape[0]
    keyw_ref[pl.ds(pl.multiple_of(row * span, span), span), :] = own_ref[...]
    keyw_ref[pl.ds(pl.multiple_of((1 - row) * span, span), span), :] = away_ref[...]
    own_lanes = pl.ds(pl.multiple_of(place_ref[2] * width, width), width)
    rows = out_ref.shape[0]
    cols = core_ref.shape[0] // rows
    core = jnp.concatenate(
        [core_ref[i * cols + j] for j in range(cols) for i in range(rows)], axis=1
    )
    attended = jnp.concatenate(
        [plain_dot(core, out_ref[i]) for i in range(out_ref.shape[0])], axis=1
    )
    wide_ref[...] = attended
    att_ref[...] = wide_ref[:, own_lanes]
    residual = single(joined(packed_ref, slice(0, tokens))) + attended
    center, inv = token_stats(residual)
    stats_ref[0] = jnp.broadcast_to(center, stats_ref.shape[1:])
    stats_ref[1] = jnp.broadcast_to(inv, stats_ref.shape[1:])
    scaled = (residual - center) * inv
    gain, bias, mix = params_ref[2:3, :], params_ref[3:4, :], params_ref[10:11, :]
    normed = scaled * gain + bias
    ffn = normed + (prev_rows(normed, keep) - normed) * mix
    wide_ref[...] = ffn
    ffn = half(ffn)
    active = jnp.maximum(plain_dot(ffn, keyw_ref[...]), 0.0)
    hidden_width = active.shape[1]
    act_ref[:, :hidden_width] = half(active * active)
    act_ref[:, hidden_width:] = half(wide_ref[:, own_lanes])
    grad_pre = half(2.0 * (hback_ref[...] + single(hgot_ref[...])) * active)
    pre_ref[...] = grad_pre
    grad_ffn = backward_dot(grad_pre, keyw_ref[...])
    gained = grad_ffn * (gain * (1.0 - mix)) + next_rows(grad_ffn * (gain * mix), keep)
    sums = column_as_rows(jnp.sum(gained, axis=1, keepdims=True), width)
    sums = sums + column_as_rows(jnp.sum(gained * scaled, axis=1, keepdims=True), width)
    block = half(rows_block(sums, width))
    for i in range(send_ref.shape[0]):
        send_ref[i, :tokens, :] = half(grad_ffn[:, i * width : (i + 1) * width])
        send_ref[i, tokens:, :] = block


def residual_backward(
    got_ref, input_ref, att_ref, stats_ref, feat_ref, doc_ref, cot_ref,
    res_ref, grad_ref, grad_half_ref, rows_ref,
):
    tokens, width = input_ref.shape
    _, _, keep = token_marks(doc_ref)
    got = sum_devices(got_ref)
    grad_ffn = got[:tokens]
    pieces = tokens // width
    means = [
        rows_as_column([got[tokens + k * pieces + i : tokens + k * pieces + i + 1] for i in range(pieces)])
        * (1.0 / EMBED_SIZE)
        for k in range(2)
    ]
    residual = input_ref[...] + att_ref[...]
    res_ref[...] = residual
    inv = stats_ref[1]
    scaled = (residual - stats_ref[0]) * inv
    gain, bias, mix = feat_ref[2:3, :], feat_ref[3:4, :], feat_ref[10:11, :]
    normed = scaled * gain + bias
    delta = prev_rows(normed, keep) - normed
    grad_normed = grad_ffn * (1.0 - mix) + next_rows(grad_ffn * mix, keep)
    rows_ref[...] = rows_block(
        [
            jnp.sum(grad_normed * scaled, axis=0, keepdims=True),
            jnp.sum(grad_normed, axis=0, keepdims=True),
            jnp.sum(grad_ffn * delta, axis=0, keepdims=True),
        ],
        width,
    )
    grad = cot_ref[...] + (grad_normed * gain - means[0] - scaled * means[1]) * inv
    grad_ref[...] = grad
    grad_half_ref[...] = half(grad)


def time_backward(
    place_ref, resg_ref, out_ref, rkv_in_ref, lows_ref, first_ref, par_ref, doc_ref,
    state_ref, solved_ref, inverse_ref, mixed_ref, turned_ref, delta_ref, scaled_ref, params_ref,
    packed_ref, proj_ref, up_ref, act0_ref, act1_ref, act2_ref, act3_ref,
    send_ref, rkv_ref, first_grad_ref, up_grad_ref,
):
    tokens, width = first_ref.shape
    act_refs = (act0_ref, act1_ref, act2_ref, act3_ref)
    marks_col, marks_row, keep = token_marks(doc_ref)
    own_rows = pl.ds(pl.multiple_of(place_ref[3] * width, width), width)
    grads = joined(resg_ref, slice(0, tokens))
    span = out_ref.shape[2]
    grad_core = sum(
        backward_dot(grads[:, i * span : (i + 1) * span], out_ref[i, own_rows, :])
        for i in range(out_ref.shape[0])
    )
    parts = (
        rkv_in_ref[0], rkv_in_ref[1], rkv_in_ref[2], first_ref[...],
        lows_ref[0], lows_ref[1], lows_ref[2], lows_ref[3],
    )
    p = [par_ref[i : i + 1, :] for i in range(8)]
    d_rkv, d_first, d_low, d_par = state_backward(
        parts, p, marks_col, marks_row, state_ref[...], solved_ref[...], inverse_ref, grad_core
    )
    first_grad_ref[...] = d_first
    rkv = [half(part) for part in d_rkv]
    for j in range(3):
        rkv_ref[j] = rkv[j]
    up_grad_ref[low_total:, :] = half(rows_block(d_par, width))
    down = joined(packed_ref, slice(tokens + 3 * pad_rows, packed_ref.shape[1]))
    low_back = []
    for i, (low, high) in enumerate(low_edges):
        low_half = half(d_low[i])
        act = act_refs[i][...]
        up_grad_ref[low:high, :] = half(outer_dot(half(act), low_half))
        back = backward_dot(low_half, up_ref[low:high, :])
        if i == 0:
            back = back * (1.0 - act * act)
        if i == 3:
            back = back * act * (1.0 - act)
        back = half(back)
        low_back.append(back)
        grad = outer_dot(back, stream(mixed_ref, turned_ref, low_streams[i]))
        for q in range(send_ref.shape[0]):
            send_ref[q, tokens + low : tokens + high, :] = half(grad[:, q * width : (q + 1) * width])
    delta = single(delta_ref[...])
    stay = moved = None
    mix_rows = []
    for j in range(6):
        back = None
        if j < 3:
            back = jnp.concatenate(
                [backward_dot(rkv[j], proj_ref[s, j]) for s in range(proj_ref.shape[0])], axis=1
            )
        if j in low_streams:
            i = low_streams.index(j)
            low, high = low_edges[i]
            term = plain_dot(low_back[i], down[low:high])
            back = term if back is None else back + term
        mix_rows.append(jnp.sum(back * delta, axis=0, keepdims=True))
        shifted = back * params_ref[4 + j : 5 + j, :]
        stay = back - shifted if stay is None else stay + (back - shifted)
        moved = shifted if moved is None else moved + shifted
    grad_normed = stay + next_rows(moved, keep)
    gained = grad_normed * params_ref[0:1, :]
    sums = column_as_rows(jnp.sum(gained, axis=1, keepdims=True), width)
    sums = sums + column_as_rows(jnp.sum(gained * scaled_ref[...], axis=1, keepdims=True), width)
    for q in range(send_ref.shape[0]):
        lanes = slice(q * width, (q + 1) * width)
        send_ref[q, :tokens, :] = half(grad_normed[:, lanes])
        send_ref[q, tokens + low_total :, :] = half(
            rows_block([row[:, lanes] for row in mix_rows] + sums, width)
        )


def input_backward(
    got_ref, input_ref, stats_ref, feat_ref, grad_ref, rows_ref,
    out_ref, small_ref,
):
    tokens, width = input_ref.shape
    got = sum_devices(got_ref)
    grad_normed = got[:tokens]
    small_ref[:low_total, :] = half(got[tokens : tokens + low_total])
    tail = got[tokens + low_total :]
    pieces = tokens // width
    means = [
        rows_as_column([tail[6 + k * pieces + i : 7 + k * pieces + i] for i in range(pieces)])
        * (1.0 / EMBED_SIZE)
        for k in range(2)
    ]
    inv = stats_ref[1]
    scaled = (input_ref[...] - stats_ref[0]) * inv
    out_ref[...] = grad_ref[...] + (
        (grad_normed * feat_ref[0:1, :] - means[0] - scaled * means[1]) * inv
    )
    rows = rows_ref[...]
    small_ref[low_total:, :] = half(
        rows_block(
            [
                jnp.sum(grad_normed * scaled, axis=0, keepdims=True),
                jnp.sum(grad_normed, axis=0, keepdims=True),
                rows[0:1],
                rows[1:2],
            ]
            + [tail[j : j + 1] for j in range(6)]
            + [rows[2:3]],
            width,
        )
    )


def channel_gradients(
    place_ref, act_own_ref, act_away_ref, pre_own_ref, pre_away_ref, side0_ref, side1_ref,
    side2_ref, side3_ref, pair0_ref, pair1_ref, pair2_ref, pair3_ref,
    key_ref, value_ref,
    ffn_ref, cot_ref,
):
    row, col, pack = place_ref[0], place_ref[1], place_ref[4]
    width = side0_ref.shape[1]
    packs = max(cot_ref.shape[0] // pack_tokens, 1)
    tokens = cot_ref.shape[0] // packs
    for k, ref in enumerate((side0_ref, side1_ref, side2_ref, side3_ref)):
        ffn_ref[:, pl.ds(pl.multiple_of((col ^ k) * width, width), width)] = ref[...]
    for k, ref in enumerate((pair0_ref, pair1_ref, pair2_ref, pair3_ref)):
        lanes = pl.ds(pl.multiple_of((col ^ k) * width, width), width)
        for m in range(packs):
            rows = pl.ds(pl.multiple_of((pack ^ m) * tokens, tokens), tokens)
            cot_ref[rows, lanes] = ref[m * tokens : (m + 1) * tokens, :]
    span = pre_own_ref.shape[1]
    for where, act, pre in (
        (row, act_own_ref, pre_own_ref), (1 - row, act_away_ref, pre_away_ref)
    ):
        block = pl.ds(pl.multiple_of(where * span, span), span)
        value_ref[block, :] = outer_dot(act[...], cot_ref[...])
        key_ref[:, block] = outer_dot(ffn_ref[...], pre[...])


def widen(
    rec_ref, key_ref, val_ref, out_ref, up_ref,
    rec_out, key_out, val_out, out_out, up_out, par_out,
):
    for source, target in (
        (rec_ref, rec_out), (key_ref, key_out), (val_ref, val_out), (out_ref, out_out)
    ):
        target[...] = single(source[...])
    rows = single(up_ref[...])
    up_out[...] = rows[:low_total]
    par_out[...] = rows[low_total : low_total + par_out.shape[0]]


def call(kernel, outs, *inputs, scratch=()):
    places = [pl.BlockSpec(memory_space=pltpu.SMEM)] if inputs[0].ndim == 1 else []
    return pl.pallas_call(
        kernel,
        in_specs=places + [pl.BlockSpec(memory_space=pltpu.VMEM)] * (len(inputs) - len(places)),
        scratch_shapes=[pltpu.VMEM(shape, dtype) for shape, dtype in scratch],
        out_shape=tuple(jax.ShapeDtypeStruct(shape, dtype) for shape, dtype in outs),
        compiler_params=pltpu.CompilerParams(vmem_limit_bytes=56 << 20),
        interpret=interpreted,
    )(*inputs)


def exchange(values, axis, offset):
    size = lax.axis_size(axis)
    return lax.ppermute(values, axis, [(i, i ^ offset) for i in range(size)])


def pick(stacked, index):
    return lax.dynamic_index_in_dim(stacked, index, 0, keepdims=False)


def power_of_two(size):
    return size & (size - 1) == 0


def gather_pieces(values, axis):
    size = lax.axis_size(axis)
    if not power_of_two(size):
        arrived = lax.all_gather(values, axis)
        return [arrived[i] for i in range(size)]
    index = lax.axis_index(axis)
    pieces = [values] + [exchange(values, axis, k) for k in range(1, size)]
    ordered = []
    for source in range(size):
        chosen = pieces[0]
        for offset in range(1, size):
            chosen = jnp.where(index ^ source == offset, pieces[offset], chosen)
        ordered.append(chosen)
    return ordered


def scatter_sum(stacked, axis):
    size = lax.axis_size(axis)
    if not power_of_two(size):
        return jnp.sum(single(lax.all_to_all(half(stacked), axis, 0, 0)), axis=0)
    index = lax.axis_index(axis)
    total = pick(stacked, index)
    for k in range(1, size):
        total = total + single(exchange(half(pick(stacked, index ^ k)), axis, k))
    return total


def small_pack_sum(values):
    if lax.axis_size("dp") != 4:
        return single(lax.psum(values, "dp"))
    near, far, both = [single(exchange(values, "dp", k)) for k in (1, 2, 3)]
    return (single(values) + near) + (far + both)


def lane_chunks(values, count):
    rows, width = values.shape
    return jnp.transpose(values.reshape(rows, count, width // count), (1, 0, 2))


def layer(
    layer_input_rows,
    first_layer_values,
    document_index,
    output_cotangent,
    feature_parameters,
    head_parameters,
    receptance_weight,
    key_weight,
    value_weight,
    output_weight,
    channel_key_weight,
    channel_value_weight,
    down_factors,
    up_factors,
):
    row_count, col_count = lax.axis_size("row"), lax.axis_size("col")
    count = row_count * col_count
    row, col = lax.axis_index("row"), lax.axis_index("col")
    tokens, width = layer_input_rows.shape
    full_width = width * count
    features, heads = feature_parameters.shape[0], head_parameters.shape[0]
    row_width = width * col_count
    hidden_width = channel_key_weight.shape[1] // row_count
    few_packs = lax.axis_size("dp") == 4
    pack = lax.axis_index("dp") if few_packs else 0
    place = jnp.stack(
        [row, col, row * col_count + col, col * row_count + row, jnp.asarray(pack, row.dtype)]
    ).astype(jnp.int32)
    f32, bf16 = jnp.float32, jnp.bfloat16
    own = (tokens, width)
    wide = (tokens, full_width)

    def row_columns(values):
        return lax.dynamic_slice_in_dim(values, row * row_width, row_width, 1)

    packed, cotangent_half, proj_own, proj_send, key_own, key_send = call(
        pack_inputs,
        [
            ((tokens + 3 * pad_rows + low_total, width), bf16),
            (own, bf16),
            ((3, row_width, width), bf16),
            ((3, row_width, width), bf16),
            ((row_width, hidden_width), bf16),
            ((row_width, hidden_width), bf16),
        ],
        place, layer_input_rows, feature_parameters, down_factors, output_cotangent,
        receptance_weight, key_weight, value_weight, channel_key_weight,
    )
    proj_away = exchange(proj_send, "row", 1)
    near = [packed] + [exchange(packed, group, k) for k in piece_offsets[1:4]]
    near[1], own_output = lax.optimization_barrier((near[1], output_weight))
    pieces = near + [exchange(piece, group, 1) for piece in near]
    output_blocks = lax.all_gather(own_output, group, axis=0, tiled=True).reshape(
        row_count, -1, output_weight.shape[1]
    )
    key_away = exchange(key_send, "row", 1)
    grad_pieces = gather_pieces(cotangent_half, "col")
    grad_blocks = jnp.concatenate(grad_pieces, axis=1)
    hidden_back = lane_chunks(backward_dot(grad_blocks, channel_value_weight), row_count)
    back_away = exchange(half(pick(hidden_back, 1 - row)), "row", 1)
    back_own = pick(hidden_back, row)

    (
        mixed, turned, delta_one, scaled_one, params, stats_one, lows,
        act0, act1, act2, act3, packed_all,
    ) = call(
        time_inputs,
        [
            ((3,) + wide, bf16),
            ((3,) + wide, bf16),
            (wide, bf16),
            (wide, f32),
            ((pad_rows, full_width), f32),
            ((2,) + own, f32),
            ((4,) + own, f32),
        ]
        + [((tokens, size), f32) for size in low_sizes]
        + [((count,) + packed.shape, bf16)],
        place, *pieces, up_factors, document_index,
    )
    core, state_out, solved, inverse, rkv, proj_weights = call(
        time_forward,
        [
            ((count,) + own, bf16),
            (own, f32),
            (own, f32),
            ((width // HEAD, tokens, tokens), f32),
            ((3,) + own, f32),
            ((row_count, 3, row_width, width), bf16),
        ],
        place, mixed, lows, proj_own, proj_away, first_layer_values, head_parameters,
        document_index,
    )
    core_all = lax.all_to_all(core, group, 0, 0)
    pair_own = cotangent_half
    if few_packs:
        pair_own = jnp.concatenate(
            [cotangent_half] + [exchange(cotangent_half, "dp", k) for k in (1, 2, 3)], axis=0
        )
    pairs = [pair_own] + [exchange(pair_own, "col", k) for k in range(1, col_count)]
    send_two, attended_own, act_side, grad_pre, stats_two = call(
        channel_forward,
        [
            ((count, tokens + pad_rows, width), bf16),
            (own, f32),
            ((tokens, hidden_width + width), bf16),
            ((tokens, hidden_width), bf16),
            ((2,) + own, f32),
        ],
        place, core_all, output_blocks, packed_all, params, document_index, key_own, key_away,
        back_own, back_away,
        scratch=[(wide, f32), ((full_width, hidden_width), bf16)],
    )
    act_all, pre_all = act_side, grad_pre
    if few_packs:
        act_all = lax.all_gather(act_side, "dp", axis=0, tiled=True)
        pre_all = lax.all_gather(grad_pre, "dp", axis=0, tiled=True)
    got_two = lax.all_to_all(send_two, group, 0, 0)
    pre_away = exchange(pre_all, "row", 1)
    residual_one, grad_residual, grad_residual_half, rows_two = call(
        residual_backward,
        [(own, f32), (own, f32), (own, bf16), ((pad_rows, width), f32)],
        got_two, layer_input_rows, attended_own, stats_two, feature_parameters, document_index,
        output_cotangent,
    )
    residual_all = lax.all_gather(grad_residual_half, group, axis=0, tiled=False)
    hidden_pieces = gather_pieces(act_side[:, :hidden_width], "row")
    hidden_blocks = jnp.concatenate(hidden_pieces, axis=1)
    block_part = plain_dot(hidden_blocks, channel_value_weight)
    block_out = residual_one + scatter_sum(lane_chunks(block_part, col_count), "col")

    send_one, rkv_half, value_first_grad, up_head_gradient = call(
        time_backward,
        [
            ((count, tokens + low_total + pad_rows, width), bf16),
            ((3,) + own, bf16),
            (own, f32),
            ((low_total + pad_rows, width), bf16),
        ],
        place, residual_all, output_blocks, rkv, lows, first_layer_values, head_parameters,
        document_index, state_out, solved, inverse, mixed, turned, delta_one, scaled_one, params,
        packed_all, proj_weights, up_factors, act0, act1, act2, act3,
    )
    rkv_pieces = gather_pieces(rkv_half, "row")
    rkv_blocks = jnp.concatenate(rkv_pieces, axis=2)
    got_one = lax.all_to_all(send_one, group, 0, 0)
    core_block = lax.dynamic_index_in_dim(
        core_all.reshape((row_count, col_count) + own), col, 1, keepdims=False
    )
    core_block = jnp.transpose(core_block, (1, 0, 2)).reshape(tokens, -1)
    residual_block = lax.dynamic_slice_in_dim(residual_all, row * col_count, col_count, 0)
    residual_block = jnp.transpose(residual_block, (1, 0, 2)).reshape(tokens, -1)
    late = (
        *[half(outer_dot(row_columns(mixed[j]), rkv_blocks[j])) for j in range(3)],
        half(outer_dot(core_block, residual_block)),
        up_head_gradient,
    )
    late = lax.psum(late, "dp")

    act_own, side_own = act_all[:, :hidden_width], act_all[:, hidden_width:]
    act_away = exchange(act_own, "row", 1)
    sides = [exchange(side_own, "col", k) for k in range(1, col_count)]
    packs_tokens = act_all.shape[0]
    channel_key_gradient, channel_value_gradient = call(
        channel_gradients,
        [(channel_key_weight.shape, f32), (channel_value_weight.shape, f32)],
        place, act_own, act_away, pre_all, pre_away, side_own, *sides, *pairs,
        scratch=[((packs_tokens, row_width), bf16), ((packs_tokens, row_width), bf16)],
    )
    if not few_packs:
        channel_key_gradient, channel_value_gradient = [
            single(lax.psum(half(piece), "dp"))
            for piece in (channel_key_gradient, channel_value_gradient)
        ]
    input_grad, small = call(
        input_backward,
        [(own, f32), ((low_total + pad_rows, width), bf16)],
        got_one, layer_input_rows, stats_one, feature_parameters, grad_residual, rows_two,
    )
    small = small_pack_sum(small)
    late = call(
        widen,
        [(piece.shape, f32) for piece in late[:4]] + [((low_total, width), f32), ((heads, width), f32)],
        *late,
    )
    return (
        block_out,
        input_grad,
        value_first_grad,
        small[low_total : low_total + features],
        late[5],
        late[0],
        late[1],
        late[2],
        late[3],
        channel_key_gradient,
        channel_value_gradient,
        small[:low_total].T,
        late[4],
    )


def solution(mesh):
    placed = (
        P("dp", ("row", "col")),
        P("dp", ("col", "row")),
        P("dp", None),
        P("dp", ("row", "col")),
        P(None, ("row", "col")),
        P(None, ("col", "row")),
        P("row", "col"),
        P("row", "col"),
        P("row", "col"),
        P("col", "row"),
        P("row", "col"),
        P("col", "row"),
        P(("row", "col"), None),
        P(None, ("col", "row")),
    )
    return jax.shard_map(
        layer,
        mesh=mesh,
        in_specs=placed,
        out_specs=(
            P("dp", ("row", "col")),
            P("dp", ("row", "col")),
            P("dp", ("col", "row")),
            P(None, ("row", "col")),
            P(None, ("col", "row")),
            P("row", "col"),
            P("row", "col"),
            P("row", "col"),
            P("col", "row"),
            P("row", "col"),
            P("col", "row"),
            P(("row", "col"), None),
            P(None, ("col", "row")),
        ),
        check_vma=False,
    )
```
